128 devices in a mesh: seq: 8 (over y, core), head: 16 (over x, z).
Axes of the slice: x: 4, y: 4, z: 4, core: 2. Of those that a mesh axis runs over, the one named last changes fastest.
Arguments:
- tokens: bfloat16 [16384, 2048], P('seq', 'head'), may hold values from -12 to 12
- w_query: bfloat16 [2048, 2048], P(None, 'head')
- w_key: bfloat16 [2048, 2048], P(None, 'head')
- w_value: bfloat16 [2048, 2048], P(None, 'head'), may hold values from -0.125 to 0.125
- w_out: bfloat16 [2048, 2048], P('head'), may hold values from -0.125 to 0.125
- cluster_id: int32 [16384, 16], P('seq', 'head'), may hold values from 0 to 63, as said below
- slot_index: int32 [16384, 16], P('seq', 'head'), may hold values from 0 to 32767, as said below
Outputs:
- mixed: bfloat16 [16384, 2048], P(('seq', 'head'))
The draws below stay inside these ranges and needn't reach their ends.
Inputs may be any that keep to these rules, and one draw needn't show every extreme that they name: `slot_index`: for each head the slots of all tokens are distinct. The slot of a token of the s-th block of 2048 tokens is b * 512 + s * 64 + j with 0 <= j < 64. For each head some block is filled by all tokens, and from each block of 2048 tokens the 512 slots that it may take in 8 consecutive blocks starting at a multiple of 8 are all filled. `cluster_id`: the cluster of a token in a head is that of its block in slot_index: consecutive blocks form runs, and a run's cluster is the index of its first block.
All inputs are finite; a program needn't handle non-finite values.
Results may differ from the reference program's by a relative error of at most 0.0053.
Values may be sent and summed in bfloat16 or wider, within the bound.
No kernel may reach another device: no remote copies, remote signals or barrier semaphores. Data moves between devices by JAX's collectives and lax.ppermute only.
A program may use at most 128 MiB of HBM per device.

```python
import jax
import jax.numpy as jnp
from jax import lax

D = 2048
HEADS = 16
HD = 128
BLOCK = 512
TOK_DEV = 2048
TOKENS = 16384
BLK_DEV = 8
MOST = 64
NBLOCK = 64
SLOTS = 32768


def routing_tables(key):
    base = jax.random.fold_in(key, 11)
    keys_all = jax.random.split(base, 5)
    seq_count = TOKENS // TOK_DEV
    npos = NBLOCK * MOST
    places = jnp.arange(npos, dtype=jnp.int32)
    block_of = places // MOST
    within = places % MOST
    full_block = jax.random.randint(keys_all[0], (HEADS, 1, 1), 0, NBLOCK)
    full_owner = jax.random.randint(keys_all[1], (HEADS, seq_count, 1), 0, seq_count)
    forced = (block_of // BLK_DEV == full_owner) | (block_of == full_block) | (block_of == 0) & (within == 0) | (block_of == NBLOCK - 1) & (within == MOST - 1)
    noise = jax.random.randint(keys_all[2], (HEADS, seq_count, npos), 0, 65536)
    scores = (forced.astype(jnp.int32) * 65536 + noise) * npos + places
    chosen = lax.top_k(scores, TOK_DEV)[1].astype(jnp.int32)
    order_keys = jax.random.randint(keys_all[3], (HEADS, seq_count, TOK_DEV), 0, 65536) * TOK_DEV + jnp.arange(TOK_DEV, dtype=jnp.int32)
    order = jnp.argsort(order_keys, axis=-1, stable=True)
    chosen = jnp.take_along_axis(chosen, order, axis=-1)
    blocks = chosen // MOST
    sources = jnp.arange(seq_count, dtype=jnp.int32)[None, :, None]
    slots = blocks * BLOCK + sources * MOST + chosen % MOST
    index = jnp.arange(NBLOCK, dtype=jnp.int32)
    starts = jax.random.randint(keys_all[4], (HEADS, NBLOCK), 0, 3) == 0
    starts = starts | (index[None, :] == 0) | (index[None, :] == NBLOCK - 1)
    labels = lax.cummax(jnp.where(starts, index[None, :], 0), axis=1)
    clusters = jnp.take_along_axis(labels, blocks.reshape(HEADS, -1), axis=1)
    return (slots.reshape(HEADS, TOKENS).T, clusters.reshape(HEADS, TOKENS).T)


def draw_slot_index(key, part):
    return routing_tables(key)[0].astype(jnp.int32)


def draw_cluster_id(key, part):
    return routing_tables(key)[1].astype(jnp.int32)


def draw_tokens(key, part):
    base = jax.random.normal(jax.random.fold_in(key, 31), (TOKENS, D), jnp.float32)
    return jnp.clip(base, -4.0, 4.0).astype(jnp.bfloat16)


def key_matrix(key):
    normal = jax.random.normal(jax.random.fold_in(key, 41), (D, HEADS * HD), jnp.float32)
    return jnp.clip(normal, -4.0, 4.0) * D ** (-0.5)


def draw_w_key(key, part):
    return key_matrix(key).astype(jnp.bfloat16)


def draw_w_query(key, part):
    normal = jax.random.normal(jax.random.fold_in(key, 43), (D, HEADS * HD), jnp.float32)
    return (jnp.clip(normal, -4.0, 4.0) * D ** (-0.5)).astype(jnp.bfloat16)


def block_levels(rng, extent, cuts, low, high):
    gain, own = 1.0, jax.random.fold_in(rng, 6)
    for dim, parts in cuts:
        draws = jnp.exp(jax.random.uniform(jax.random.fold_in(own, dim), (parts,), jnp.float32, low / len(cuts), high / len(cuts)))
        gain = gain * jnp.repeat(draws, extent[dim] // parts).reshape([-1 if axis == dim else 1 for axis in range(len(extent))])
    return gain


def gaussian(stream_key, shape, width, most, pieces=(), kind=jnp.bfloat16):
    values = jax.random.normal(stream_key, shape, jnp.float32) * width
    if len(pieces) > 0:
        values = block_levels(stream_key, shape, pieces, -0.22, 0.18) * values
    return jnp.clip(values, min=-most, max=most).astype(kind)


def setup_inputs(seed: int = 0) -> dict:
    key_list = jax.random.split(jax.random.key(seed), 8)
    return {
        "tokens": draw_tokens(jax.random.fold_in(key_list[7], 71), 0),
        "w_query": draw_w_query(jax.random.fold_in(key_list[7], 71), 0),
        "w_key": draw_w_key(jax.random.fold_in(key_list[7], 71), 0),
        "w_value": gaussian(key_list[3], (D, HEADS * HD), D ** -0.5, 0.125, ((1, 16),)),
        "w_out": gaussian(key_list[4], (HEADS * HD, D), (HEADS * HD) ** -0.5, 0.125, ((0, 16),)),
        "cluster_id": draw_cluster_id(jax.random.fold_in(key_list[7], 71), 0),
        "slot_index": draw_slot_index(jax.random.fold_in(key_list[7], 71), 0),
    }


def attend_block(items):
    own_rows, prev_rows, own_pos, prev_pos, own_code, prev_code = items
    query = own_rows[:, :HD].astype(jnp.float32)
    keys = jnp.concatenate([prev_rows[:, HD:2 * HD], own_rows[:, HD:2 * HD]], 0).astype(jnp.float32)
    values = jnp.concatenate([prev_rows[:, 2 * HD:], own_rows[:, 2 * HD:]], 0)
    key_pos = jnp.concatenate([prev_pos, own_pos], 0)
    key_code = jnp.concatenate([prev_code, own_code], 0)
    scores = jnp.einsum("qd,kd->qk", query, keys, precision=lax.Precision.HIGHEST) * (HD ** -0.5)
    allowed = (key_code[None, :] == own_code[:, None]) & (key_code[None, :] > 0) & (key_pos[None, :] <= own_pos[:, None])
    masked = jnp.where(allowed, scores, jnp.float32(-1e30))
    largest = jnp.max(masked, axis=1, keepdims=True)
    expon = jnp.exp(masked - largest)
    weights = (expon / jnp.sum(expon, axis=1, keepdims=True)).astype(jnp.bfloat16)
    return jnp.dot(weights, values, preferred_element_type=jnp.float32).astype(jnp.bfloat16)


def reference(tokens, w_query, w_key, w_value, w_out, cluster_id, slot_index):
    query = jnp.dot(tokens, w_query, preferred_element_type=jnp.float32).astype(jnp.bfloat16)
    keyed = jnp.dot(tokens, w_key, preferred_element_type=jnp.float32).astype(jnp.bfloat16)
    valued = jnp.dot(tokens, w_value, preferred_element_type=jnp.float32).astype(jnp.bfloat16)
    positions = jnp.arange(TOKENS, dtype=jnp.int32)

    def one_head(head):
        start = (head * HD).astype(jnp.int32)
        packed = jnp.concatenate([lax.dynamic_slice_in_dim(query, start, HD, 1), lax.dynamic_slice_in_dim(keyed, start, HD, 1), lax.dynamic_slice_in_dim(valued, start, HD, 1)], 1)
        slots = slot_index[:, head]
        layout = jnp.zeros((SLOTS, 3 * HD), jnp.bfloat16).at[slots].set(packed)
        codes = jnp.zeros((SLOTS,), jnp.int32).at[slots].set(cluster_id[:, head] + 1)
        places = jnp.zeros((SLOTS,), jnp.int32).at[slots].set(positions)
        layout = layout.reshape(NBLOCK, BLOCK, 3 * HD)
        codes = codes.reshape(NBLOCK, BLOCK)
        places = places.reshape(NBLOCK, BLOCK)
        prev_layout = jnp.concatenate([jnp.zeros((1, BLOCK, 3 * HD), jnp.bfloat16), layout[:-1]], 0)
        prev_codes = jnp.concatenate([jnp.zeros((1, BLOCK), jnp.int32), codes[:-1]], 0)
        prev_places = jnp.concatenate([jnp.zeros((1, BLOCK), jnp.int32), places[:-1]], 0)
        attended = lax.map(attend_block, (layout, prev_layout, places, prev_places, codes, prev_codes))
        return attended.reshape(SLOTS, HD)[slots]

    per_head = lax.map(one_head, jnp.arange(HEADS, dtype=jnp.int32))
    attended = jnp.transpose(per_head, (1, 0, 2)).reshape(TOKENS, HEADS * HD)
    summed = jnp.dot(attended, w_out, preferred_element_type=jnp.float32)
    return (summed + tokens.astype(jnp.float32)).astype(jnp.bfloat16)
```

```python
import functools
import math

import jax
import jax.numpy as jnp
from jax import lax
from jax.experimental import pallas as pl
from jax.experimental.pallas import tpu as pltpu
from jax.sharding import Mesh, PartitionSpec as P

HD = 128
BLOCK = 512
TOK = 2048
HALF = TOK // 2
SEQ = 8
SIDE = 4
HEADS = 16
WIDTH = 2048
BLK = 8
MOST = 64
ROWS = SEQ * BLK * MOST
EMPTY = 1 << 30
POS = 1 << 14
OFFSETS = (0, -1, 1, 2)
SCALE = HD ** (-0.5) * math.log2(math.e)
BF = jnp.bfloat16
F32 = jnp.float32


VMEM = pl.BlockSpec(memory_space=pltpu.VMEM)
SMEM = pl.BlockSpec(memory_space=pltpu.SMEM)


def params():
    return pltpu.CompilerParams(vmem_limit_bytes=60 * 1024 * 1024)


def ring(by):
    return [(i, (i + by) % SIDE) for i in range(SIDE)]


def ring_gather(piece, axis):
    back = lax.ppermute(piece, axis, ring(1))
    ahead = lax.ppermute(piece, axis, ring(-1))
    half = piece.shape[0] // 2
    far_low = lax.ppermute(back[:half], axis, ring(1))
    far_high = lax.ppermute(ahead[half:], axis, ring(-1))
    return back, ahead, far_low, far_high


def gather_tokens(part, first, second):
    back, ahead, far_low, far_high = ring_gather(part, first)
    mine = jnp.concatenate([part, back, ahead, far_low, far_high], 0)
    return (mine,) + ring_gather(mine, second)


def wrap(index, by):
    return lax.rem(index + (by + SIDE), SIDE)


def columns_of(place_ref, swapped, outer, inner):
    x, z = place_ref[0], place_ref[1]
    if swapped:
        return wrap(x, outer) * SIDE + wrap(z, inner)
    return wrap(x, inner) * SIDE + wrap(z, outer)


def fill_weights(place_ref, weights, target, swapped, outers, inners_of):
    row = 0
    for outer in outers:
        for inner in inners_of:
            src = pl.multiple_of(columns_of(place_ref, swapped, outer, inner) * HD, HD)
            for n, w in enumerate(weights):
                target[row : row + HD, n * HD : (n + 1) * HD] = w[pl.ds(src, HD), :]
            row += HD


TILE = 256


def project_near(place_ref, wq, wk, wv, a0, a1, a2, b0, b1, b2, acc_ref, wa, wb):
    weights = (wq, wk, wv)
    fill_weights(place_ref, weights, wa, False, OFFSETS[:3], OFFSETS)
    fill_weights(place_ref, weights, wb, True, OFFSETS[:3], OFFSETS)
    for base, pieces, w in ((0, (a0, a1, a2), wa), (HALF, (b0, b1, b2), wb)):
        def step(i, carry, base=base, pieces=pieces, w=w):
            lhs = jnp.concatenate(
                [
                    p[pl.ds(pl.multiple_of(n * HALF + i * TILE, TILE), TILE), :]
                    for p in pieces
                    for n in range(SIDE)
                ],
                1,
            )
            acc_ref[pl.ds(pl.multiple_of(base + i * TILE, TILE), TILE), :] = jnp.dot(
                lhs, w[...], preferred_element_type=F32
            )
            return carry

        lax.fori_loop(0, HALF // TILE, step, 0)


def scatter_rows(index_ref, src, pad, count):
    def step(i, carry):
        for k in range(16):
            t = i * 16 + k
            pad[pl.ds(index_ref[t], 1), :] = src[pl.ds(t, 1), :]
        return carry

    lax.fori_loop(0, count // 16, step, 0)


def project_far(
    place_ref, index_ref, wq, wk, wv, acc, a0, a1, b0, b1, kv_ref, q_ref, wa, wb, rows, pad
):
    weights = (wq, wk, wv)
    fill_weights(place_ref, weights, wa, False, OFFSETS[3:], OFFSETS)
    fill_weights(place_ref, weights, wb, True, OFFSETS[3:], OFFSETS)
    for base, pieces, w in ((0, (a0, a1), wa), (HALF, (b0, b1), wb)):
        def step(i, carry, base=base, pieces=pieces, w=w):
            lhs = jnp.concatenate(
                [
                    p[pl.ds(pl.multiple_of(n * HALF + i * TILE, TILE), TILE), :]
                    for p in pieces
                    for n in range(SIDE // 2)
                ],
                1,
            )
            at = pl.ds(pl.multiple_of(base + i * TILE, TILE), TILE)
            total = acc[at, :] + jnp.dot(lhs, w[...], preferred_element_type=F32)
            total = total.astype(BF).astype(F32)
            q_ref[at, :] = total[:, :HD]
            rows[at, :] = total[:, HD:]
            return carry

        lax.fori_loop(0, HALF // TILE, step, 0)
    pad[...] = jnp.zeros_like(pad)
    scatter_rows(index_ref, rows, pad, TOK)
    kv_ref[...] = pad[...].astype(BF)


def place_query(index_ref, rows, out_ref, pad):
    pad[...] = jnp.zeros_like(pad)
    scatter_rows(index_ref, rows, pad, TOK)
    out_ref[...] = pad[...].astype(BF)


def place_values(index_ref, value_ref, out_ref):
    def clear(i, carry):
        for k in range(32):
            out_ref[i * 32 + k] = EMPTY
        return carry

    lax.fori_loop(0, ROWS // 32, clear, 0)

    def step(i, carry):
        for k in range(16):
            t = i * 16 + k
            out_ref[index_ref[t]] = value_ref[t]
        return carry

    lax.fori_loop(0, TOK // 16, step, 0)


QT = 128


def attend(q_ref, kv_ref, halo_ref, key_val, query_val, out_ref):
    for b in range(BLK):
        for i in range(BLOCK // QT):
            srcs = QT // MOST * (i + 1)
            n = QT * (i + 1)
            lo = QT // MOST * i
            query = q_ref[lo:srcs, b].reshape(QT, HD)
            own = kv_ref[:srcs, b].reshape(n, 2 * HD)
            before = (halo_ref[:srcs] if b == 0 else kv_ref[:srcs, b - 1]).reshape(n, 2 * HD)
            mine = query_val[i * QT : (i + 1) * QT, b : b + 1]
            base = mine & ~(POS - 1)
            parts = []
            for rows, line in ((before, b), (own, b + 1)):
                score = lax.dot_general(
                    query, rows[:, :HD], (((1,), (1,)), ((), ())), preferred_element_type=F32
                )
                theirs = key_val[line : line + 1, :n]
                parts.append(jnp.where((theirs <= mine) & (theirs >= base), score, F32(-1e30)))
            largest = jnp.maximum(
                jnp.max(parts[0], axis=1, keepdims=True), jnp.max(parts[1], axis=1, keepdims=True)
            )
            total = None
            mixed = None
            for part, rows in zip(parts, (before, own)):
                expon = jnp.exp2((part - largest) * F32(SCALE))
                add = jnp.sum(expon, axis=1, keepdims=True)
                prod = jnp.dot(expon.astype(BF), rows[:, HD:], preferred_element_type=F32)
                total = add if total is None else total + add
                mixed = prod if mixed is None else mixed + prod
            out_ref[lo:srcs, b] = (mixed / total).astype(BF).reshape(srcs - lo, MOST, HD)


def take_rows(index_ref, rows_ref, out_ref, wide, taken):
    wide[...] = rows_ref[...].astype(F32)

    def step(i, carry):
        for k in range(16):
            t = i * 16 + k
            taken[pl.ds(t, 1), :] = wide[pl.ds(index_ref[t], 1), :]
        return carry

    lax.fori_loop(0, TOK // 16, step, 0)
    out_ref[...] = taken[...].astype(BF)


def pick_own(place_ref, a0, a1, a2, a3, a4, b0, b1, b2, b3, b4, out_ref):
    head = place_ref[0] * SIDE + place_ref[1]
    per = HALF // HD

    def copy(pieces, swapped, row):
        for outer, group in zip(OFFSETS, (pieces[0], pieces[1], pieces[2], pieces[3:])):
            for n, inner in enumerate(OFFSETS):
                if outer == 2:
                    ref, at = group[n // 2], n % 2
                else:
                    ref, at = group, n
                col = pl.multiple_of(columns_of(place_ref, swapped, outer, inner) * HD, HD)
                out_ref[:, pl.ds(col, HD)] = ref[
                    pl.ds(pl.multiple_of(at * HALF + row * HD, HD), HD), :
                ]

    @pl.when(head < per)
    def _():
        copy((a0, a1, a2, a3, a4), False, head)

    @pl.when(head >= per)
    def _():
        copy((b0, b1, b2, b3, b4), True, head - per)


def combine(core_ref, rows_ref, near_ref, far_ref, own_ref, out_ref):
    lhs = jnp.concatenate([rows_ref[h] for h in range(HEADS)], 1)
    half = WIDTH // 2
    core = core_ref[0]
    step = 256
    for ref, which in ((near_ref, core), (far_ref, 1 - core)):
        for n in range(half // step):
            col = pl.multiple_of(which * half + n * step, step)
            total = jnp.dot(
                lhs, ref[:, n * step : (n + 1) * step], preferred_element_type=F32
            )
            out_ref[:, pl.ds(col, step)] = (
                total + own_ref[:, pl.ds(col, step)].astype(F32)
            ).astype(BF)


def local(tokens, w_query, w_key, w_value, w_out, cluster_id, slot_index):
    x, z, seq = lax.axis_index("hx"), lax.axis_index("hz"), lax.axis_index("seq")
    place = jnp.stack([x, z]).astype(jnp.int32)
    core = lax.rem(seq, 2)

    pieces_a = gather_tokens(tokens[:HALF], "hx", "hz")
    pieces_b = gather_tokens(tokens[HALF:], "hz", "hx")

    slots = slot_index.reshape(TOK)
    index = (slots // BLOCK) * MOST + slots % MOST
    value = cluster_id.reshape(TOK) * POS + seq * TOK + jnp.arange(TOK, dtype=jnp.int32)
    values = pl.pallas_call(
        place_values,
        out_shape=jax.ShapeDtypeStruct((ROWS,), jnp.int32),
        in_specs=[SMEM, SMEM],
        out_specs=SMEM,
        name="place_values",
        cost_estimate=pl.CostEstimate(flops=0, bytes_accessed=12 << 20, transcendentals=0),
    )(index, value)
    values = lax.all_to_all(values.reshape(SEQ, BLK * MOST), "seq", 0, 0, tiled=True)
    values = values.reshape(SEQ, BLK, MOST).transpose(1, 0, 2).reshape(BLK, BLOCK)
    forward = [(i, i + 1) for i in range(SEQ - 1)]
    line = lax.ppermute(values[BLK - 1 :], "seq", forward)
    line = jnp.where(seq == 0, EMPTY, line)
    key_val = jnp.concatenate([line, values], 0)
    query_val = values.T

    weights = (w_query, w_key, w_value)
    near = pl.pallas_call(
        project_near,
        out_shape=jax.ShapeDtypeStruct((TOK, 3 * HD), F32),
        in_specs=[SMEM] + [VMEM] * 9,
        out_specs=VMEM,
        scratch_shapes=[pltpu.VMEM((12 * HD, 3 * HD), BF)] * 2,
        compiler_params=params(),
        name="project_near",
        cost_estimate=pl.CostEstimate(
            flops=2 * TOK * 12 * HD * 3 * HD, bytes_accessed=10 << 20, transcendentals=0
        ),
    )(place, *weights, *pieces_a[:3], *pieces_b[:3])
    sent_kv, rows_q = pl.pallas_call(
        project_far,
        out_shape=(
            jax.ShapeDtypeStruct((ROWS, 2 * HD), BF),
            jax.ShapeDtypeStruct((TOK, HD), F32),
        ),
        in_specs=[SMEM, SMEM] + [VMEM] * 8,
        out_specs=(VMEM, VMEM),
        scratch_shapes=[pltpu.VMEM((4 * HD, 3 * HD), BF)] * 2
        + [pltpu.VMEM((TOK, 2 * HD), F32), pltpu.VMEM((ROWS, 2 * HD), F32)],
        compiler_params=params(),
        name="project_far",
        cost_estimate=pl.CostEstimate(
            flops=2 * TOK * 4 * HD * 3 * HD, bytes_accessed=20 << 20, transcendentals=0
        ),
    )(place, index, *weights, near, *pieces_a[3:], *pieces_b[3:])
    got_kv = lax.all_to_all(
        sent_kv.reshape(SEQ, BLK, MOST, 2 * HD), "seq", 0, 0, tiled=True
    )
    sent_q = pl.pallas_call(
        place_query,
        out_shape=jax.ShapeDtypeStruct((ROWS, HD), BF),
        in_specs=[SMEM, VMEM],
        out_specs=VMEM,
        scratch_shapes=[pltpu.VMEM((ROWS, HD), F32)],
        compiler_params=params(),
        name="place_query",
        cost_estimate=pl.CostEstimate(flops=0, bytes_accessed=8 << 20, transcendentals=0),
    )(index, rows_q)
    got_q = lax.all_to_all(sent_q.reshape(SEQ, BLK, MOST, HD), "seq", 0, 0, tiled=True)
    own = pl.pallas_call(
        pick_own,
        out_shape=jax.ShapeDtypeStruct((HD, WIDTH), BF),
        in_specs=[SMEM] + [VMEM] * 10,
        out_specs=VMEM,
        compiler_params=params(),
        name="pick_own",
        cost_estimate=pl.CostEstimate(flops=0, bytes_accessed=1 << 20, transcendentals=0),
    )(place, *pieces_a, *pieces_b)

    w_half = lax.dynamic_slice_in_dim(w_out, core * (WIDTH // 2), WIDTH // 2, 1)
    w_half, _ = lax.optimization_barrier((w_half, rows_q))
    w_near = lax.all_to_all(
        jnp.broadcast_to(w_half[None], (HEADS, HD, WIDTH // 2)), ("hx", "hz"), 0, 0, tiled=True
    ).reshape(WIDTH, WIDTH // 2)
    w_far = lax.ppermute(w_near, "seq", [(i, i ^ 1) for i in range(SEQ)])

    halo = lax.ppermute(got_kv[:, BLK - 1], "seq", forward)
    attended = pl.pallas_call(
        attend,
        out_shape=jax.ShapeDtypeStruct((SEQ, BLK, MOST, HD), BF),
        in_specs=[VMEM] * 5,
        out_specs=VMEM,
        compiler_params=params(),
        name="attend",
        cost_estimate=pl.CostEstimate(
            flops=4 * BLK * BLOCK * 2 * BLOCK * HD,
            bytes_accessed=5 << 20,
            transcendentals=BLK * BLOCK * 2 * BLOCK,
        ),
    )(got_q, got_kv, halo, key_val, query_val)
    back = lax.all_to_all(attended, "seq", 0, 0, tiled=True).reshape(ROWS, HD)
    taken = pl.pallas_call(
        take_rows,
        out_shape=jax.ShapeDtypeStruct((TOK, HD), BF),
        in_specs=[SMEM, VMEM],
        out_specs=VMEM,
        scratch_shapes=[pltpu.VMEM((ROWS, HD), F32), pltpu.VMEM((TOK, HD), F32)],
        compiler_params=params(),
        name="take_rows",
        cost_estimate=pl.CostEstimate(flops=0, bytes_accessed=8 << 20, transcendentals=0),
    )(index, back)
    all_heads = lax.all_to_all(
        taken.reshape(HEADS, HD, HD), ("hx", "hz"), 0, 0, tiled=True
    )
    return pl.pallas_call(
        combine,
        out_shape=jax.ShapeDtypeStruct((HD, WIDTH), BF),
        in_specs=[SMEM] + [VMEM] * 4,
        out_specs=VMEM,
        compiler_params=params(),
        name="combine",
        cost_estimate=pl.CostEstimate(
            flops=2 * HD * WIDTH * WIDTH, bytes_accessed=10 << 20, transcendentals=0
        ),
    )(core.reshape(1), all_heads, w_near, w_far, own)


def solution(mesh):
    grid = Mesh(mesh.devices.reshape(SEQ, SIDE, SIDE), ("seq", "hx", "hz"))
    head = ("hx", "hz")
    in_specs = (
        P("seq", head),
        P(None, head),
        P(None, head),
        P(None, head),
        P(head, None),
        P("seq", head),
        P("seq", head),
    )
    out_specs = P(("seq", "hx", "hz"), None)
    return jax.shard_map(local, mesh=grid, in_specs=in_specs, out_specs=out_specs, check_vma=False)
```

```python
import math

import jax
import jax.numpy as jnp
from jax import lax
from jax.experimental import pallas as pl
from jax.experimental.pallas import tpu as pltpu
from jax.sharding import Mesh, PartitionSpec as P

HD = 128
BLOCK = 512
TOK = 2048
HALF = TOK // 2
SEQ = 8
SIDE = 4
HEADS = 16
WIDTH = 2048
BLK = 8
MOST = 64
ROWS = SEQ * BLK * MOST
SENT = BLK + BLK // 2 + 1
EMPTY = 1 << 30
POS = 1 << 14
OFFSETS = (0, -1, 1, 2)
SCALE = HD ** (-0.5) * math.log2(math.e)
BF = jnp.bfloat16
F32 = jnp.float32


VMEM = pl.BlockSpec(memory_space=pltpu.VMEM)
SMEM = pl.BlockSpec(memory_space=pltpu.SMEM)


def params(mib):
    return pltpu.CompilerParams(vmem_limit_bytes=mib * 1024 * 1024)


def ring(by):
    return [(i, (i + by) % SIDE) for i in range(SIDE)]


def ring_gather(piece, axis):
    back = lax.ppermute(piece, axis, ring(1))
    ahead = lax.ppermute(piece, axis, ring(-1))
    half = piece.shape[0] // 2
    far_low = lax.ppermute(back[:half], axis, ring(1))
    far_high = lax.ppermute(ahead[half:], axis, ring(-1))
    return back, ahead, far_low, far_high


def gather_near(part, first, second):
    back, ahead, far_low, far_high = ring_gather(part, first)
    low = jnp.concatenate([part, back], 0)
    high = jnp.concatenate([ahead, far_low, far_high], 0)
    back_low = lax.ppermute(low, second, ring(1))
    ahead_low = lax.ppermute(low, second, ring(-1))
    ahead_high = lax.ppermute(high, second, ring(-1))
    back_high = lax.ppermute(high, second, ring(1))
    return low, high, back_low, back_high, ahead_low, ahead_high


def gather_far(near, second):
    return lax.ppermute(near[2], second, ring(1)), lax.ppermute(near[5], second, ring(-1))


def wrap(index, by):
    return lax.rem(index + (by + SIDE), SIDE)


def slice_of(place_ref, swapped, outer, inner):
    x, z = place_ref[0], place_ref[1]
    if swapped:
        return wrap(x, outer) * SIDE + wrap(z, inner)
    return wrap(x, inner) * SIDE + wrap(z, outer)


def piece_list(refs, outers):
    return [
        (refs[2 * n + m // 2], m % 2, outer, inner)
        for n, outer in enumerate(outers)
        for m, inner in enumerate(OFFSETS)
    ]


def fill_weights(place_ref, weights, target, swapped, outers):
    row = 0
    for outer in outers:
        for inner in OFFSETS:
            src = pl.multiple_of(slice_of(place_ref, swapped, outer, inner) * HD, HD)
            for n, w in enumerate(weights):
                target[row : row + HD, n * HD : (n + 1) * HD] = w[pl.ds(src, HD), :]
            row += HD


def pick_own(place_ref, halves, own_ref):
    head = place_ref[0] * SIDE + place_ref[1]
    per = HALF // HD
    for swapped, pieces in halves:
        row = head - per if swapped else head

        @pl.when((head >= per) if swapped else (head < per))
        def _():
            for ref, at, outer, inner in pieces:
                col = pl.multiple_of(slice_of(place_ref, swapped, outer, inner) * HD, HD)
                rows = pl.multiple_of(at * HALF + row * HD, HD)
                own_ref[:, pl.ds(col, HD)] = ref[pl.ds(rows, HD), :]


TILE = 256


def multiply(pieces, base, w, finish):
    def step(i, carry):
        lhs = jnp.concatenate(
            [
                ref[pl.ds(pl.multiple_of(at * HALF + i * TILE, TILE), TILE), :]
                for ref, at, _, _ in pieces
            ],
            1,
        )
        rows = pl.ds(pl.multiple_of(base + i * TILE, TILE), TILE)
        finish(rows, jnp.dot(lhs, w[...], preferred_element_type=F32))
        return carry

    lax.fori_loop(0, HALF // TILE, step, 0)


def project_near(place_ref, wq, wk, wv, *refs):
    acc_ref, own_ref, wa, wb = refs[12:]
    a, b = piece_list(refs[:6], OFFSETS[:3]), piece_list(refs[6:12], OFFSETS[:3])
    fill_weights(place_ref, (wq, wk, wv), wa, False, OFFSETS[:3])
    fill_weights(place_ref, (wq, wk, wv), wb, True, OFFSETS[:3])

    def finish(rows, total):
        acc_ref[rows, :] = total

    multiply(a, 0, wa, finish)
    multiply(b, HALF, wb, finish)
    pick_own(place_ref, ((False, a), (True, b)), own_ref)


def scatter_rows(index_ref, src, pad):
    def step(i, carry):
        for k in range(16):
            t = i * 16 + k
            pad[pl.ds(index_ref[t], 1), :] = src[pl.ds(t, 1), :]
        return carry

    lax.fori_loop(0, TOK // 16, step, 0)


def project_far(
    place_ref, index_ref, wq, wk, wv, acc, own_in, a0, a1, b0, b1, out_ref, own_ref, wa, wb, rows, pad
):
    a, b = piece_list((a0, a1), OFFSETS[3:]), piece_list((b0, b1), OFFSETS[3:])
    fill_weights(place_ref, (wq, wk, wv), wa, False, OFFSETS[3:])
    fill_weights(place_ref, (wq, wk, wv), wb, True, OFFSETS[3:])

    def finish(at, total):
        rows[at, :] = (acc[at, :] + total).astype(BF).astype(F32)

    multiply(a, 0, wa, finish)
    multiply(b, HALF, wb, finish)
    own_ref[...] = own_in[...]
    pick_own(place_ref, ((False, a), (True, b)), own_ref)
    pad[...] = jnp.zeros_like(pad)
    scatter_rows(index_ref, rows, pad)

    def pack(o, carry):
        base = o * (BLK * MOST)

        def line(b):
            return pl.ds(pl.multiple_of(base + b * MOST, MOST), MOST)

        for b in range(BLK):
            out_ref[o, b] = pad[line(b), HD:].astype(BF)
        for b in range(0, BLK, 2):
            out_ref[o, BLK + b // 2] = jnp.concatenate(
                [pad[line(b), :HD], pad[line(b + 1), :HD]], 1
            ).astype(BF)
        return carry

    lax.fori_loop(0, SEQ, pack, 0)
    out_ref[0, SENT - 1] = jnp.zeros((MOST, 2 * HD), BF)
    for o in range(1, SEQ):
        out_ref[o, SENT - 1] = out_ref[o - 1, BLK - 1]


def place_values(index_ref, value_ref, out_ref):
    def clear(i, carry):
        for k in range(32):
            out_ref[i * 32 + k] = EMPTY
        return carry

    lax.fori_loop(0, ROWS // 32, clear, 0)

    def step(i, carry):
        for k in range(16):
            t = i * 16 + k
            out_ref[index_ref[t]] = value_ref[t]
        return carry

    lax.fori_loop(0, TOK // 16, step, 0)


QT = 128


def attend(got, key_own, key_before, query_val, out_ref):
    ones = jnp.ones((BLOCK, HD), BF)
    for b in range(BLK):
        for i in range(BLOCK // QT):
            srcs = QT // MOST * (i + 1)
            n = QT * (i + 1)
            lo = QT // MOST * i
            half = b % 2 * HD
            query = got[lo:srcs, BLK + b // 2, :, half : half + HD].reshape(QT, HD)
            own = got[:srcs, b].reshape(n, 2 * HD)
            before = got[:srcs, SENT - 1 if b == 0 else b - 1].reshape(n, 2 * HD)
            mine = query_val[i * QT : (i + 1) * QT, b : b + 1]
            parts = []
            for rows, line in ((before, key_before), (own, key_own)):
                score = lax.dot_general(
                    query, rows[:, :HD], (((1,), (1,)), ((), ())), preferred_element_type=F32
                )
                parts.append(jnp.where(line[b : b + 1, :n] <= mine, score, F32(-1e30)))
            largest = jnp.maximum(
                jnp.max(parts[0], axis=1, keepdims=True), jnp.max(parts[1], axis=1, keepdims=True)
            )
            mixed = None
            for part, rows in zip(parts, (before, own)):
                expon = jnp.exp2((part - largest) * F32(SCALE)).astype(BF)
                prod = jnp.dot(
                    expon,
                    jnp.concatenate([rows[:, HD:], ones[:n]], 1),
                    preferred_element_type=F32,
                )
                mixed = prod if mixed is None else mixed + prod
            done = (mixed[:, :HD] / mixed[:, HD:]).astype(BF)
            out_ref[lo:srcs, b] = done.reshape(srcs - lo, MOST, HD)


def take_rows(index_ref, rows_ref, out_ref, wide, taken):
    wide[...] = rows_ref[...].astype(F32)

    def step(i, carry):
        for k in range(16):
            t = i * 16 + k
            taken[pl.ds(t, 1), :] = wide[pl.ds(index_ref[t], 1), :]
        return carry

    lax.fori_loop(0, TOK // 16, step, 0)
    out_ref[...] = taken[...].astype(BF)


COLS = 256


def combine(place_ref, rows_ref, *refs):
    near, far = refs[:5], refs[5:10]
    own_ref, out_ref, lhs = refs[10:]
    n = pl.program_id(0)

    @pl.when(n == 0)
    def _():
        for k, outer in enumerate(OFFSETS):
            for m, inner in enumerate(OFFSETS):
                h = slice_of(place_ref, False, outer, inner)
                col = (k * SIDE + m) * HD
                lhs[:, col : col + HD] = rows_ref[h]

    core = place_ref[2]
    for group, which in ((near, core), (far, 1 - core)):
        total, row = None, 0
        for w in group:
            depth = w.shape[0]
            prod = jnp.dot(lhs[:, row : row + depth], w[...], preferred_element_type=F32)
            total = prod if total is None else total + prod
            row += depth
        col = pl.ds(pl.multiple_of(which * (WIDTH // 2) + n * COLS, COLS), COLS)
        out_ref[:, col] = (total + own_ref[:, col].astype(F32)).astype(BF)


def estimate(flops, mib):
    return pl.CostEstimate(flops=flops, bytes_accessed=mib << 20, transcendentals=0)


def shape(dims, kind):
    return jax.ShapeDtypeStruct(dims, kind)


def local(tokens, w_query, w_key, w_value, w_out, cluster_id, slot_index):
    x, z, seq = lax.axis_index("hx"), lax.axis_index("hz"), lax.axis_index("seq")
    core = lax.rem(seq, 2)
    place = jnp.stack([x, z, core]).astype(jnp.int32)

    slots = slot_index.reshape(TOK)
    index = (slots // BLOCK) * MOST + slots % MOST
    value = cluster_id.reshape(TOK) * POS + seq * TOK + jnp.arange(TOK, dtype=jnp.int32)

    near_a = gather_near(tokens[:HALF], "hx", "hz")
    near_b = gather_near(tokens[HALF:], "hz", "hx")

    values = pl.pallas_call(
        place_values,
        out_shape=shape((ROWS,), jnp.int32),
        in_specs=[SMEM, SMEM],
        out_specs=SMEM,
        name="place_values",
        cost_estimate=estimate(0, 12),
    )(index, value).reshape(SEQ, BLK, MOST)
    halo = jnp.concatenate(
        [jnp.full((1, 1, MOST), EMPTY, jnp.int32), values[: SEQ - 1, BLK - 1 :]], 0
    )
    values = jnp.concatenate([halo, values], 1).reshape(SEQ, (BLK + 1) * MOST)
    values = lax.all_to_all(values, "seq", 0, 0, tiled=True)
    values = values.reshape(SEQ, BLK + 1, MOST).transpose(1, 0, 2).reshape(BLK + 1, BLOCK)
    key_own = values[1:]
    base = jnp.min(key_own, axis=1, keepdims=True) & ~(POS - 1)
    key_before = jnp.where(values[:BLK] >= base, values[:BLK], EMPTY)
    query_val = key_own.T

    weights = (w_query, w_key, w_value)
    acc, own = pl.pallas_call(
        project_near,
        out_shape=(shape((TOK, 3 * HD), F32), shape((HD, WIDTH), BF)),
        in_specs=[SMEM] + [VMEM] * 15,
        out_specs=(VMEM, VMEM),
        scratch_shapes=[pltpu.VMEM((12 * HD, 3 * HD), BF)] * 2,
        compiler_params=params(20),
        name="project_near",
        cost_estimate=estimate(2 * TOK * 12 * HD * 3 * HD, 10),
    )(place, *weights, *near_a, *near_b)
    far_a = gather_far(near_a, "hz")
    far_b = gather_far(near_b, "hx")
    sent, own = pl.pallas_call(
        project_far,
        out_shape=(shape((SEQ, SENT, MOST, 2 * HD), BF), shape((HD, WIDTH), BF)),
        in_specs=[SMEM, SMEM] + [VMEM] * 9,
        out_specs=(VMEM, VMEM),
        scratch_shapes=[pltpu.VMEM((4 * HD, 3 * HD), BF)] * 2
        + [pltpu.VMEM((TOK, 3 * HD), F32), pltpu.VMEM((ROWS, 3 * HD), F32)],
        compiler_params=params(28),
        name="project_far",
        cost_estimate=estimate(2 * TOK * 4 * HD * 3 * HD, 24),
    )(place, index, *weights, acc, own, *far_a, *far_b)
    got = lax.all_to_all(sent, "seq", 0, 0, tiled=True)

    w_half = lax.dynamic_slice_in_dim(w_out, core * (WIDTH // 2), WIDTH // 2, 1)
    w_half, _ = lax.optimization_barrier((w_half, own))
    w_row = jnp.concatenate((w_half,) + ring_gather(w_half, "hx"), 0)
    w_near = (w_row,) + ring_gather(w_row, "hz")
    w_far = tuple(lax.ppermute(w, "seq", [(i, i ^ 1) for i in range(SEQ)]) for w in w_near)

    attended = pl.pallas_call(
        attend,
        out_shape=shape((SEQ, BLK, MOST, HD), BF),
        in_specs=[VMEM] * 4,
        out_specs=VMEM,
        compiler_params=params(16),
        name="attend",
        cost_estimate=estimate(4 * BLK * BLOCK * 2 * BLOCK * HD, 8),
    )(got, key_own, key_before, query_val)
    back = lax.all_to_all(attended, "seq", 0, 0, tiled=True).reshape(ROWS, HD)
    taken = pl.pallas_call(
        take_rows,
        out_shape=shape((TOK, HD), BF),
        in_specs=[SMEM, VMEM],
        out_specs=VMEM,
        scratch_shapes=[pltpu.VMEM((ROWS, HD), F32), pltpu.VMEM((TOK, HD), F32)],
        compiler_params=params(10),
        name="take_rows",
        cost_estimate=estimate(0, 8),
    )(index, back)
    all_heads = lax.all_to_all(
        taken.reshape(HEADS, HD, HD), ("hx", "hz"), 0, 0, tiled=True
    )
    whole = lambda *dims: pl.BlockSpec(dims, lambda n: (0,) * len(dims))
    w_specs = [
        pl.BlockSpec((depth, COLS), lambda n: (0, n)) for depth in (512, 512, 512, 256, 256)
    ]
    return pl.pallas_call(
        combine,
        grid=(WIDTH // 2 // COLS,),
        out_shape=shape((HD, WIDTH), BF),
        in_specs=[SMEM, whole(HEADS, HD, HD)] + w_specs * 2 + [whole(HD, WIDTH)],
        out_specs=whole(HD, WIDTH),
        scratch_shapes=[pltpu.VMEM((HD, WIDTH), BF)],
        compiler_params=params(16),
        name="combine",
        cost_estimate=estimate(2 * HD * WIDTH * WIDTH, 10),
    )(place, all_heads, *w_near, *w_far, own)


def solution(mesh):
    grid = Mesh(mesh.devices.reshape(SEQ, SIDE, SIDE), ("seq", "hx", "hz"))
    head = ("hx", "hz")
    in_specs = (
        P("seq", head),
        P(None, head),
        P(None, head),
        P(None, head),
        P(head, None),
        P("seq", head),
        P("seq", head),
    )
    out_specs = P(("seq", "hx", "hz"), None)
    return jax.shard_map(local, mesh=grid, in_specs=in_specs, out_specs=out_specs, check_vma=False)
```

```python
import math

import jax
import jax.numpy as jnp
from jax import lax
from jax.experimental import pallas as pl
from jax.experimental.pallas import tpu as pltpu
from jax.sharding import Mesh, PartitionSpec as P

HD = 128
BLOCK = 512
TOK = 2048
HALF = TOK // 2
SEQ = 8
SIDE = 4
HEADS = 16
WIDTH = 2048
BLK = 8
MOST = 64
ROWS = SEQ * BLK * MOST
SENT = BLK + BLK // 2 + 1
LINE = 4
EMPTY = 1 << 30
POS = 1 << 14
OFFSETS = (0, -1, 1, 2)
SCALE = HD ** (-0.5) * math.log2(math.e)
BF = jnp.bfloat16
F32 = jnp.float32


VMEM = pl.BlockSpec(memory_space=pltpu.VMEM)
SMEM = pl.BlockSpec(memory_space=pltpu.SMEM)
HBM = pl.BlockSpec(memory_space=pltpu.HBM)


def params(mib):
    return pltpu.CompilerParams(vmem_limit_bytes=mib * 1024 * 1024)


def ring(by):
    return [(i, (i + by) % SIDE) for i in range(SIDE)]


def ring_gather(piece, axis):
    back = lax.ppermute(piece, axis, ring(1))
    ahead = lax.ppermute(piece, axis, ring(-1))
    half = piece.shape[0] // 2
    far_low = lax.ppermute(back[:half], axis, ring(1))
    far_high = lax.ppermute(ahead[half:], axis, ring(-1))
    return back, ahead, far_low, far_high


def gather_near(part, first, second):
    back, ahead, far_low, far_high = ring_gather(part, first)
    low = jnp.concatenate([part, back], 0)
    high = jnp.concatenate([ahead, far_low, far_high], 0)
    back_low = lax.ppermute(low, second, ring(1))
    ahead_low = lax.ppermute(low, second, ring(-1))
    ahead_high = lax.ppermute(high, second, ring(-1))
    back_high = lax.ppermute(high, second, ring(1))
    return low, high, back_low, back_high, ahead_low, ahead_high


def gather_far(near, second):
    return lax.ppermute(near[2], second, ring(1)), lax.ppermute(near[5], second, ring(-1))


def wrap(index, by):
    return lax.rem(index + (by + SIDE), SIDE)


def slice_of(place_ref, swapped, outer, inner):
    x, z = place_ref[0], place_ref[1]
    if swapped:
        return wrap(x, outer) * SIDE + wrap(z, inner)
    return wrap(x, inner) * SIDE + wrap(z, outer)


def piece_list(refs, outers):
    return [
        (refs[2 * n + m // 2], m % 2, outer, inner)
        for n, outer in enumerate(outers)
        for m, inner in enumerate(OFFSETS)
    ]


def fill_weights(place_ref, weights, target, swapped, outers):
    row = 0
    for outer in outers:
        for inner in OFFSETS:
            src = pl.multiple_of(slice_of(place_ref, swapped, outer, inner) * HD, HD)
            for n, w in enumerate(weights):
                target[row : row + HD, n * HD : (n + 1) * HD] = w[pl.ds(src, HD), :]
            row += HD


def pick_own(place_ref, halves, own_ref):
    head = place_ref[0] * SIDE + place_ref[1]
    per = HALF // HD
    for swapped, pieces in halves:
        row = head - per if swapped else head

        @pl.when((head >= per) if swapped else (head < per))
        def _():
            for ref, at, outer, inner in pieces:
                col = pl.multiple_of(slice_of(place_ref, swapped, outer, inner) * HD, HD)
                rows = pl.multiple_of(at * HALF + row * HD, HD)
                own_ref[:, pl.ds(col, HD)] = ref[pl.ds(rows, HD), :]


TILE = 256


def multiply(pieces, base, w, finish):
    def step(i, carry):
        lhs = jnp.concatenate(
            [
                ref[pl.ds(pl.multiple_of(at * HALF + i * TILE, TILE), TILE), :]
                for ref, at, _, _ in pieces
            ],
            1,
        )
        rows = pl.ds(pl.multiple_of(base + i * TILE, TILE), TILE)
        finish(rows, jnp.dot(lhs, w[...], preferred_element_type=F32))
        return carry

    lax.fori_loop(0, HALF // TILE, step, 0)


def project_near(place_ref, wq, wk, wv, *refs):
    acc_ref, own_ref, wa, wb = refs[12:]
    a, b = piece_list(refs[:6], OFFSETS[:3]), piece_list(refs[6:12], OFFSETS[:3])
    fill_weights(place_ref, (wq, wk, wv), wa, False, OFFSETS[:3])
    fill_weights(place_ref, (wq, wk, wv), wb, True, OFFSETS[:3])

    def finish(rows, total):
        acc_ref[rows, :] = total

    multiply(a, 0, wa, finish)
    multiply(b, HALF, wb, finish)
    pick_own(place_ref, ((False, a), (True, b)), own_ref)


def scatter_rows(index_ref, src, pad):
    def step(i, carry):
        for k in range(16):
            t = i * 16 + k
            pad[index_ref[t]] = src[t]
        return carry

    lax.fori_loop(0, TOK // 16, step, 0)


def project_far(
    place_ref, index_ref, wq, wk, wv, acc, own_in, a0, a1, b0, b1, out_ref, own_ref, wa, wb, rows, pad, full, sems
):
    a, b = piece_list((a0, a1), OFFSETS[3:]), piece_list((b0, b1), OFFSETS[3:])
    fill_weights(place_ref, (wq, wk, wv), wa, False, OFFSETS[3:])
    fill_weights(place_ref, (wq, wk, wv), wb, True, OFFSETS[3:])

    def finish(at, total):
        total = (acc[at, :] + total).astype(BF).astype(F32)
        twice = pl.multiple_of(at.start * (ROWS // TOK), TILE)
        pad[pl.ds(twice, TILE * ROWS // TOK)] = jnp.zeros((TILE * ROWS // TOK, LINE, HD), F32)
        flat = rows.reshape(TOK * LINE, HD)
        start = pl.multiple_of(at.start * LINE, LINE)
        for k in range(3):
            flat[pl.ds(start + k, TILE, stride=LINE), :] = total[:, k * HD : (k + 1) * HD]

    multiply(a, 0, wa, finish)
    multiply(b, HALF, wb, finish)
    own_ref[...] = own_in[...]
    pick_own(place_ref, ((False, a), (True, b)), own_ref)
    scatter_rows(index_ref, rows, pad)

    def send(o):
        return pltpu.make_async_copy(full.at[o], out_ref.at[o], sems.at[o])

    flat = pad.reshape(ROWS * LINE, HD)
    for o in range(SEQ):
        base = o * (BLK * MOST)

        def line(b, *kinds):
            at = (base + b * MOST) * LINE
            return jnp.concatenate(
                [flat[pl.ds(at + k, MOST, stride=LINE), :] for k in kinds], 1
            ).astype(BF)

        for b in range(BLK):
            full[o, b] = line(b, 1, 2)
        for b in range(0, BLK, 2):
            full[o, BLK + b // 2] = jnp.concatenate([line(b, 0), line(b + 1, 0)], 1)
        full[o, SENT - 1] = line(-1, 1, 2) if o else jnp.zeros((MOST, 2 * HD), BF)
        send(o).start()
    for o in range(SEQ):
        send(o).wait()


def place_values(index_ref, value_ref, empty_ref, out_ref):
    pltpu.sync_copy(empty_ref, out_ref)

    def step(i, carry):
        for k in range(16):
            t = i * 16 + k
            out_ref[index_ref[t]] = value_ref[t]
        return carry

    lax.fori_loop(0, TOK // 16, step, 0)


QT = 128


def attend(got, key_own, key_before, query_val, out_ref, full, sems):
    def send(b):
        return pltpu.make_async_copy(full.at[:, b], out_ref.at[:, b], sems.at[b])

    ones = jnp.ones((BLOCK, HD), BF)
    for b in range(BLK):
        for i in range(BLOCK // QT):
            srcs = QT // MOST * (i + 1)
            n = QT * (i + 1)
            lo = QT // MOST * i
            half = b % 2 * HD
            query = got[lo:srcs, BLK + b // 2, :, half : half + HD].reshape(QT, HD)
            own = got[:srcs, b].reshape(n, 2 * HD)
            before = got[:srcs, SENT - 1 if b == 0 else b - 1].reshape(n, 2 * HD)
            mine = query_val[i * QT : (i + 1) * QT, b : b + 1]
            parts = []
            for rows, line in ((before, key_before), (own, key_own)):
                score = lax.dot_general(
                    query, rows[:, :HD], (((1,), (1,)), ((), ())), preferred_element_type=F32
                )
                parts.append(jnp.where(line[b : b + 1, :n] <= mine, score, F32(-1e30)))
            largest = jnp.maximum(
                jnp.max(parts[0], axis=1, keepdims=True), jnp.max(parts[1], axis=1, keepdims=True)
            )
            mixed = None
            for part, rows in zip(parts, (before, own)):
                expon = jnp.exp2((part - largest) * F32(SCALE)).astype(BF)
                prod = jnp.dot(
                    expon,
                    jnp.concatenate([rows[:, HD:], ones[:n]], 1),
                    preferred_element_type=F32,
                )
                mixed = prod if mixed is None else mixed + prod
            done = (mixed[:, :HD] / mixed[:, HD:]).astype(BF)
            full[lo:srcs, b] = done.reshape(srcs - lo, MOST, HD)
        send(b).start()
    for b in range(BLK):
        send(b).wait()


def take_rows(index_ref, rows_ref, out_ref, wide, taken):
    wide.reshape(ROWS, HD)[...] = rows_ref[...].astype(F32)

    def step(i, carry):
        for k in range(16):
            t = i * 16 + k
            taken[t] = wide[index_ref[t]]
        return carry

    lax.fori_loop(0, TOK // 16, step, 0)
    out_ref[...] = taken.reshape(TOK, HD)[...].astype(BF)


COLS = 256


def combine(place_ref, rows_ref, *refs):
    near, far = refs[:5], refs[5:10]
    own_ref, out_ref, lhs = refs[10:]
    n = pl.program_id(0)

    @pl.when(n == 0)
    def _():
        for k, outer in enumerate(OFFSETS):
            for m, inner in enumerate(OFFSETS):
                h = slice_of(place_ref, False, outer, inner)
                col = (k * SIDE + m) * HD
                lhs[:, col : col + HD] = rows_ref[h]

    core = place_ref[2]
    for group, which in ((near, core), (far, 1 - core)):
        total, row = None, 0
        for w in group:
            depth = w.shape[0]
            prod = jnp.dot(lhs[:, row : row + depth], w[...], preferred_element_type=F32)
            total = prod if total is None else total + prod
            row += depth
        col = pl.ds(pl.multiple_of(which * (WIDTH // 2) + n * COLS, COLS), COLS)
        out_ref[:, col] = (total + own_ref[:, col].astype(F32)).astype(BF)


def estimate(flops, mib):
    return pl.CostEstimate(flops=flops, bytes_accessed=mib << 20, transcendentals=0)


def shape(dims, kind):
    return jax.ShapeDtypeStruct(dims, kind)


def local(tokens, w_query, w_key, w_value, w_out, cluster_id, slot_index):
    x, z, seq = lax.axis_index("hx"), lax.axis_index("hz"), lax.axis_index("seq")
    core = lax.rem(seq, 2)
    place = jnp.stack([x, z, core]).astype(jnp.int32)

    slots = slot_index.reshape(TOK)
    index = (slots // BLOCK) * MOST + slots % MOST
    value = cluster_id.reshape(TOK) * POS + seq * TOK + jnp.arange(TOK, dtype=jnp.int32)

    near_a = gather_near(tokens[:HALF], "hx", "hz")
    near_b = gather_near(tokens[HALF:], "hz", "hx")
    tied, _ = lax.optimization_barrier((index, near_a[1]))
    values = pl.pallas_call(
        place_values,
        out_shape=shape((ROWS,), jnp.int32),
        in_specs=[SMEM, SMEM, pl.BlockSpec(memory_space=pl.ANY)],
        out_specs=SMEM,
        name="place_values",
        cost_estimate=estimate(0, 12),
    )(tied, value, jnp.full((ROWS,), EMPTY, jnp.int32)).reshape(SEQ, BLK, MOST)
    halo = jnp.concatenate(
        [jnp.full((1, 1, MOST), EMPTY, jnp.int32), values[: SEQ - 1, BLK - 1 :]], 0
    )
    values = jnp.concatenate([halo, values], 1).reshape(SEQ, (BLK + 1) * MOST)
    values = lax.all_to_all(values, "seq", 0, 0, tiled=True)
    last, values = lax.optimization_barrier((near_b[5], values))
    near_b = near_b[:5] + (last,)
    values = values.reshape(SEQ, BLK + 1, MOST).transpose(1, 0, 2).reshape(BLK + 1, BLOCK)
    key_own = values[1:]
    base = jnp.min(key_own, axis=1, keepdims=True) & ~(POS - 1)
    key_before = jnp.where(values[:BLK] >= base, values[:BLK], EMPTY)
    query_val = key_own.T

    weights = (w_query, w_key, w_value)
    acc, own = pl.pallas_call(
        project_near,
        out_shape=(shape((TOK, 3 * HD), F32), shape((HD, WIDTH), BF)),
        in_specs=[SMEM] + [VMEM] * 15,
        out_specs=(VMEM, VMEM),
        scratch_shapes=[pltpu.VMEM((12 * HD, 3 * HD), BF)] * 2,
        compiler_params=params(20),
        name="project_near",
        cost_estimate=estimate(2 * TOK * 12 * HD * 3 * HD, 10),
    )(place, *weights, *near_a, *near_b)
    far_a = gather_far(near_a, "hz")
    far_b = gather_far(near_b, "hx")
    sent, own = pl.pallas_call(
        project_far,
        out_shape=(pltpu.HBM((SEQ, SENT, MOST, 2 * HD), BF), shape((HD, WIDTH), BF)),
        in_specs=[SMEM, SMEM] + [VMEM] * 9,
        out_specs=(HBM, VMEM),
        scratch_shapes=[pltpu.VMEM((4 * HD, 3 * HD), BF)] * 2
        + [
            pltpu.VMEM((TOK, LINE, HD), F32),
            pltpu.VMEM((ROWS, LINE, HD), F32),
            pltpu.VMEM((SEQ, SENT, MOST, 2 * HD), BF),
            pltpu.SemaphoreType.DMA((SEQ,)),
        ],
        compiler_params=params(40),
        name="project_far",
        cost_estimate=estimate(2 * TOK * 4 * HD * 3 * HD, 24),
    )(place, index, *weights, acc, own, *far_a, *far_b)
    got = lax.all_to_all(sent, "seq", 0, 0, tiled=True)

    w_half = lax.dynamic_slice_in_dim(w_out, core * (WIDTH // 2), WIDTH // 2, 1)
    w_half, _ = lax.optimization_barrier((w_half, own))
    w_row = jnp.concatenate((w_half,) + ring_gather(w_half, "hx"), 0)
    w_near = (w_row,) + ring_gather(w_row, "hz")
    w_far = tuple(lax.ppermute(w, "seq", [(i, i ^ 1) for i in range(SEQ)]) for w in w_near)

    attended = pl.pallas_call(
        attend,
        out_shape=pltpu.HBM((SEQ, BLK, MOST, HD), BF),
        in_specs=[VMEM] * 4,
        out_specs=HBM,
        scratch_shapes=[
            pltpu.VMEM((SEQ, BLK, MOST, HD), BF),
            pltpu.SemaphoreType.DMA((BLK,)),
        ],
        compiler_params=params(16),
        name="attend",
        cost_estimate=estimate(4 * BLK * BLOCK * 2 * BLOCK * HD, 8),
    )(got, key_own, key_before, query_val)
    back = lax.all_to_all(attended, "seq", 0, 0, tiled=True).reshape(ROWS, HD)
    taken = pl.pallas_call(
        take_rows,
        out_shape=shape((TOK, HD), BF),
        in_specs=[SMEM, VMEM],
        out_specs=VMEM,
        scratch_shapes=[pltpu.VMEM((ROWS, 1, HD), F32), pltpu.VMEM((TOK, 1, HD), F32)],
        compiler_params=params(10),
        name="take_rows",
        cost_estimate=estimate(0, 8),
    )(index, back)
    all_heads = lax.all_to_all(
        taken.reshape(HEADS, HD, HD), ("hx", "hz"), 0, 0, tiled=True
    )
    whole = lambda *dims: pl.BlockSpec(dims, lambda n: (0,) * len(dims))
    w_specs = [
        pl.BlockSpec((depth, COLS), lambda n: (0, n)) for depth in (512, 512, 512, 256, 256)
    ]
    return pl.pallas_call(
        combine,
        grid=(WIDTH // 2 // COLS,),
        out_shape=shape((HD, WIDTH), BF),
        in_specs=[SMEM, whole(HEADS, HD, HD)] + w_specs * 2 + [whole(HD, WIDTH)],
        out_specs=whole(HD, WIDTH),
        scratch_shapes=[pltpu.VMEM((HD, WIDTH), BF)],
        compiler_params=params(16),
        name="combine",
        cost_estimate=estimate(2 * HD * WIDTH * WIDTH, 10),
    )(place, all_heads, *w_near, *w_far, own)


def solution(mesh):
    grid = Mesh(mesh.devices.reshape(SEQ, SIDE, SIDE), ("seq", "hx", "hz"))
    head = ("hx", "hz")
    in_specs = (
        P("seq", head),
        P(None, head),
        P(None, head),
        P(None, head),
        P(head, None),
        P("seq", head),
        P("seq", head),
    )
    out_specs = P(("seq", "hx", "hz"), None)
    return jax.shard_map(local, mesh=grid, in_specs=in_specs, out_specs=out_specs, check_vma=False)
```

```python
import math

import jax
import jax.numpy as jnp
from jax import lax
from jax.experimental import pallas as pl
from jax.experimental.pallas import tpu as pltpu
from jax.sharding import Mesh, PartitionSpec as P

HD = 128
BLOCK = 512
TOK = 2048
HALF = TOK // 2
SEQ = 8
SIDE = 4
HEADS = 16
WIDTH = 2048
BLK = 8
MOST = 64
ROWS = SEQ * BLK * MOST
TOLD = (BLK + BLK // 2 + 1) * MOST
SENT = TOLD + 16
LINE = 4
EMPTY = 1 << 20
POS = 1 << 14
OFFSETS = (0, -1, 1, 2)
SCALE = HD ** (-0.5) * math.log2(math.e)
BF = jnp.bfloat16
F32 = jnp.float32


VMEM = pl.BlockSpec(memory_space=pltpu.VMEM)
SMEM = pl.BlockSpec(memory_space=pltpu.SMEM)
HBM = pl.BlockSpec(memory_space=pltpu.HBM)


def params(mib):
    return pltpu.CompilerParams(vmem_limit_bytes=mib * 1024 * 1024)


def ring(by):
    return [(i, (i + by) % SIDE) for i in range(SIDE)]


def ring_gather(piece, axis):
    back = lax.ppermute(piece, axis, ring(1))
    ahead = lax.ppermute(piece, axis, ring(-1))
    half = piece.shape[0] // 2
    far_low = lax.ppermute(back[:half], axis, ring(1))
    far_high = lax.ppermute(ahead[half:], axis, ring(-1))
    return back, ahead, far_low, far_high


def gather_near(part, first, second):
    back, ahead, far_low, far_high = ring_gather(part, first)
    low = jnp.concatenate([part, back], 0)
    high = jnp.concatenate([ahead, far_low, far_high], 0)
    back_low = lax.ppermute(low, second, ring(1))
    ahead_low = lax.ppermute(low, second, ring(-1))
    ahead_high = lax.ppermute(high, second, ring(-1))
    back_high = lax.ppermute(high, second, ring(1))
    return low, high, back_low, back_high, ahead_low, ahead_high


def gather_far(near, second):
    return lax.ppermute(near[2], second, ring(1)), lax.ppermute(near[5], second, ring(-1))


def wrap(index, by):
    return lax.rem(index + (by + SIDE), SIDE)


def slice_of(place_ref, swapped, outer, inner):
    x, z = place_ref[0], place_ref[1]
    if swapped:
        return wrap(x, outer) * SIDE + wrap(z, inner)
    return wrap(x, inner) * SIDE + wrap(z, outer)


def piece_list(refs, outers):
    return [
        (refs[2 * n + m // 2], m % 2, outer, inner)
        for n, outer in enumerate(outers)
        for m, inner in enumerate(OFFSETS)
    ]


def fill_weights(place_ref, weights, target, swapped, outers):
    row = 0
    for outer in outers:
        for inner in OFFSETS:
            src = pl.multiple_of(slice_of(place_ref, swapped, outer, inner) * HD, HD)
            for n, w in enumerate(weights):
                target[row : row + HD, n * HD : (n + 1) * HD] = w[pl.ds(src, HD), :]
            row += HD


def pick_own(place_ref, halves, own_ref):
    head = place_ref[0] * SIDE + place_ref[1]
    per = HALF // HD
    for swapped, pieces in halves:
        row = head - per if swapped else head

        @pl.when((head >= per) if swapped else (head < per))
        def _():
            for ref, at, outer, inner in pieces:
                col = pl.multiple_of(slice_of(place_ref, swapped, outer, inner) * HD, HD)
                rows = pl.multiple_of(at * HALF + row * HD, HD)
                own_ref[:, pl.ds(col, HD)] = ref[pl.ds(rows, HD), :]


TILE = 256


def multiply(pieces, base, w, finish):
    def step(i, carry):
        lhs = jnp.concatenate(
            [
                ref[pl.ds(pl.multiple_of(at * HALF + i * TILE, TILE), TILE), :]
                for ref, at, _, _ in pieces
            ],
            1,
        )
        rows = pl.ds(pl.multiple_of(base + i * TILE, TILE), TILE)
        finish(rows, jnp.dot(lhs, w[...], preferred_element_type=F32))
        return carry

    lax.fori_loop(0, HALF // TILE, step, 0)


def project_near(place_ref, wq, wk, wv, *refs):
    acc_ref, own_ref, wa, wb = refs[12:]
    a, b = piece_list(refs[:6], OFFSETS[:3]), piece_list(refs[6:12], OFFSETS[:3])
    fill_weights(place_ref, (wq, wk, wv), wa, False, OFFSETS[:3])
    fill_weights(place_ref, (wq, wk, wv), wb, True, OFFSETS[:3])

    def finish(rows, total):
        acc_ref[rows, :] = total

    multiply(a, 0, wa, finish)
    multiply(b, HALF, wb, finish)
    pick_own(place_ref, ((False, a), (True, b)), own_ref)


def scatter_rows(index_ref, src, pad):
    def step(i, carry):
        for k in range(16):
            t = i * 16 + k
            pad[index_ref[t]] = src[t]
        return carry

    lax.fori_loop(0, TOK // 16, step, 0)


def project_far(
    place_ref, index_ref, wq, wk, wv, told, acc, own_in, a0, a1, b0, b1, out_ref, own_ref, wa, wb, rows, pad, full, sems
):
    a, b = piece_list((a0, a1), OFFSETS[3:]), piece_list((b0, b1), OFFSETS[3:])
    fill_weights(place_ref, (wq, wk, wv), wa, False, OFFSETS[3:])
    fill_weights(place_ref, (wq, wk, wv), wb, True, OFFSETS[3:])

    def finish(at, total):
        total = (acc[at, :] + total).astype(BF).astype(F32)
        twice = pl.multiple_of(at.start * (ROWS // TOK), TILE)
        pad[pl.ds(twice, TILE * ROWS // TOK)] = jnp.zeros((TILE * ROWS // TOK, LINE, HD), F32)
        flat = rows.reshape(TOK * LINE, HD)
        start = pl.multiple_of(at.start * LINE, LINE)
        for k in range(3):
            flat[pl.ds(start + k, TILE, stride=LINE), :] = total[:, k * HD : (k + 1) * HD]

    multiply(a, 0, wa, finish)
    multiply(b, HALF, wb, finish)
    own_ref[...] = own_in[...]
    pick_own(place_ref, ((False, a), (True, b)), own_ref)
    scatter_rows(index_ref, rows, pad)

    def send(o):
        return pltpu.make_async_copy(full.at[o], out_ref.at[o], sems.at[o])

    flat = pad.reshape(ROWS * LINE, HD)
    for o in range(SEQ):
        base = o * (BLK * MOST)

        def line(b, *kinds):
            at = (base + b * MOST) * LINE
            return jnp.concatenate(
                [flat[pl.ds(at + k, MOST, stride=LINE), :] for k in kinds], 1
            ).astype(BF)

        def put(n, value):
            full[o, n * MOST : (n + 1) * MOST, :] = value

        for b in range(BLK):
            put(b, line(b, 1, 2))
        for b in range(0, BLK, 2):
            put(BLK + b // 2, jnp.concatenate([line(b, 0), line(b + 1, 0)], 1))
        put(BLK + BLK // 2, line(-1, 1, 2) if o else jnp.zeros((MOST, 2 * HD), BF))
        full[o, TOLD:, :] = told[o]
        send(o).start()
    for o in range(SEQ):
        send(o).wait()


def place_values(index_ref, value_ref, empty_ref, out_ref):
    pltpu.sync_copy(empty_ref, out_ref)

    def step(i, carry):
        for k in range(16):
            t = i * 16 + k
            out_ref[index_ref[t]] = value_ref[t]
        return carry

    lax.fori_loop(0, TOK // 16, step, 0)


QT = 128


def attend(got, out_ref, keys, full, sems):
    def send(b):
        return pltpu.make_async_copy(full.at[:, b], out_ref.at[:, b], sems.at[b])

    def rows_of(n, srcs=SEQ):
        return got[:srcs, n * MOST : (n + 1) * MOST, :].reshape(srcs * MOST, 2 * HD)

    digits = got[:, TOLD:, :].astype(F32)
    value = digits[:, 0:3] + digits[:, 3:6] * 256.0 + digits[:, 6:9] * 65536.0
    lines = []
    for b in range(-1, BLK):
        row, at = (2, 0) if b < 0 else (b // 4, b % 4 * MOST)
        lines.append(
            jnp.concatenate([value[s, row : row + 1, at : at + MOST] for s in range(SEQ)], 1)
        )
    column = jnp.concatenate(lines[1:], 0).T
    last = BLK + BLK // 2
    for n in range(BLK + 1):
        keys[n] = rows_of(last if n == 0 else n - 1)[:, :HD].T

    ones = jnp.ones((BLOCK, HD), BF)
    for b in range(BLK):
        base = jnp.floor(jnp.min(lines[b + 1], axis=1, keepdims=True) * (1.0 / POS)) * POS
        earlier = jnp.where(lines[b] >= base, lines[b], float(EMPTY))
        for i in range(BLOCK // QT):
            srcs = QT // MOST * (i + 1)
            n = QT * (i + 1)
            lo = QT // MOST * i
            half = b % 2 * HD
            query = rows_of(BLK + b // 2, srcs)[lo * MOST :, half : half + HD]
            mine = column[i * QT : (i + 1) * QT, b : b + 1]
            parts = []
            for which, line in ((b, earlier), (b + 1, lines[b + 1])):
                score = jnp.dot(query, keys[which, :, :n], preferred_element_type=F32)
                parts.append(jnp.where(line[:, :n] <= mine, score, F32(-1e30)))
            largest = jnp.maximum(
                jnp.max(parts[0], axis=1, keepdims=True), jnp.max(parts[1], axis=1, keepdims=True)
            )
            mixed = None
            for part, which in zip(parts, (last if b == 0 else b - 1, b)):
                expon = jnp.exp2((part - largest) * F32(SCALE)).astype(BF)
                prod = jnp.dot(
                    expon,
                    jnp.concatenate([rows_of(which, srcs)[:, HD:], ones[:n]], 1),
                    preferred_element_type=F32,
                )
                mixed = prod if mixed is None else mixed + prod
            done = (mixed[:, :HD] / mixed[:, HD:]).astype(BF)
            full[lo:srcs, b] = done.reshape(srcs - lo, MOST, HD)
        send(b).start()
    for b in range(BLK):
        send(b).wait()


def take_rows(index_ref, rows_ref, out_ref, wide, taken):
    wide.reshape(ROWS, HD)[...] = rows_ref[...].astype(F32)

    def step(i, carry):
        for k in range(16):
            t = i * 16 + k
            taken[t] = wide[index_ref[t]]
        return carry

    lax.fori_loop(0, TOK // 16, step, 0)
    out_ref[...] = taken.reshape(TOK, HD)[...].astype(BF)


COLS = 256


def combine(place_ref, rows_ref, *refs):
    near, far = refs[:5], refs[5:10]
    own_ref, out_ref, lhs = refs[10:]
    n = pl.program_id(0)

    @pl.when(n == 0)
    def _():
        for k, outer in enumerate(OFFSETS):
            for m, inner in enumerate(OFFSETS):
                h = slice_of(place_ref, False, outer, inner)
                col = (k * SIDE + m) * HD
                lhs[:, col : col + HD] = rows_ref[h]

    core = place_ref[2]
    for group, which in ((near, core), (far, 1 - core)):
        total, row = None, 0
        for w in group:
            depth = w.shape[0]
            prod = jnp.dot(lhs[:, row : row + depth], w[...], preferred_element_type=F32)
            total = prod if total is None else total + prod
            row += depth
        col = pl.ds(pl.multiple_of(which * (WIDTH // 2) + n * COLS, COLS), COLS)
        out_ref[:, col] = (total + own_ref[:, col].astype(F32)).astype(BF)


def estimate(flops, mib):
    return pl.CostEstimate(flops=flops, bytes_accessed=mib << 20, transcendentals=0)


def shape(dims, kind):
    return jax.ShapeDtypeStruct(dims, kind)


def local(tokens, w_query, w_key, w_value, w_out, cluster_id, slot_index):
    x, z, seq = lax.axis_index("hx"), lax.axis_index("hz"), lax.axis_index("seq")
    core = lax.rem(seq, 2)
    place = jnp.stack([x, z, core]).astype(jnp.int32)

    slots = slot_index.reshape(TOK)
    index = (slots // BLOCK) * MOST + slots % MOST
    value = cluster_id.reshape(TOK) * POS + seq * TOK + jnp.arange(TOK, dtype=jnp.int32)

    near_a = gather_near(tokens[:HALF], "hx", "hz")
    near_b = gather_near(tokens[HALF:], "hz", "hx")
    tied, _ = lax.optimization_barrier((index, near_a[1]))
    values = pl.pallas_call(
        place_values,
        out_shape=shape((ROWS,), jnp.int32),
        in_specs=[SMEM, SMEM, pl.BlockSpec(memory_space=pl.ANY)],
        out_specs=SMEM,
        name="place_values",
        cost_estimate=estimate(0, 12),
    )(tied, value, jnp.full((ROWS,), EMPTY, jnp.int32)).reshape(SEQ, BLK, MOST)
    halo = jnp.concatenate(
        [jnp.full((1, MOST), EMPTY, jnp.int32), values[: SEQ - 1, BLK - 1]], 0
    )
    halo = jnp.pad(halo, ((0, 0), (0, 2 * HD - MOST)))[:, None]
    values = jnp.concatenate([values.reshape(SEQ, 2, 2 * HD), halo], 1)
    told = jnp.concatenate([values & 255, (values >> 8) & 255, values >> 16], 1)
    told = jnp.pad(told, ((0, 0), (0, SENT - TOLD - 9), (0, 0))).astype(BF)
    last, told = lax.optimization_barrier((near_b[5], told))
    near_b = near_b[:5] + (last,)

    weights = (w_query, w_key, w_value)
    acc, own = pl.pallas_call(
        project_near,
        out_shape=(shape((TOK, 3 * HD), F32), shape((HD, WIDTH), BF)),
        in_specs=[SMEM] + [VMEM] * 15,
        out_specs=(VMEM, VMEM),
        scratch_shapes=[pltpu.VMEM((12 * HD, 3 * HD), BF)] * 2,
        compiler_params=params(20),
        name="project_near",
        cost_estimate=estimate(2 * TOK * 12 * HD * 3 * HD, 10),
    )(place, *weights, *near_a, *near_b)
    far_a = gather_far(near_a, "hz")
    far_b = gather_far(near_b, "hx")
    sent, own = pl.pallas_call(
        project_far,
        out_shape=(pltpu.HBM((SEQ, SENT, 2 * HD), BF), shape((HD, WIDTH), BF)),
        in_specs=[SMEM, SMEM] + [VMEM] * 10,
        out_specs=(HBM, VMEM),
        scratch_shapes=[pltpu.VMEM((4 * HD, 3 * HD), BF)] * 2
        + [
            pltpu.VMEM((TOK, LINE, HD), F32),
            pltpu.VMEM((ROWS, LINE, HD), F32),
            pltpu.VMEM((SEQ, SENT, 2 * HD), BF),
            pltpu.SemaphoreType.DMA((SEQ,)),
        ],
        compiler_params=params(28),
        name="project_far",
        cost_estimate=estimate(2 * TOK * 4 * HD * 3 * HD, 24),
    )(place, index, *weights, told, acc, own, *far_a, *far_b)
    got = lax.all_to_all(sent, "seq", 0, 0, tiled=True)

    w_half = lax.dynamic_slice_in_dim(w_out, core * (WIDTH // 2), WIDTH // 2, 1)
    w_half, _ = lax.optimization_barrier((w_half, own))
    w_row = jnp.concatenate((w_half,) + ring_gather(w_half, "hx"), 0)
    w_near = (w_row,) + ring_gather(w_row, "hz")
    w_far = tuple(lax.ppermute(w, "seq", [(i, i ^ 1) for i in range(SEQ)]) for w in w_near)

    attended = pl.pallas_call(
        attend,
        out_shape=pltpu.HBM((SEQ, BLK, MOST, HD), BF),
        in_specs=[VMEM],
        out_specs=HBM,
        scratch_shapes=[
            pltpu.VMEM((BLK + 1, HD, BLOCK), BF),
            pltpu.VMEM((SEQ, BLK, MOST, HD), BF),
            pltpu.SemaphoreType.DMA((BLK,)),
        ],
        compiler_params=params(16),
        name="attend",
        cost_estimate=estimate(4 * BLK * BLOCK * 2 * BLOCK * HD, 8),
    )(got)
    back = lax.all_to_all(attended, "seq", 0, 0, tiled=True).reshape(ROWS, HD)
    taken = pl.pallas_call(
        take_rows,
        out_shape=shape((TOK, HD), BF),
        in_specs=[SMEM, VMEM],
        out_specs=VMEM,
        scratch_shapes=[pltpu.VMEM((ROWS, 1, HD), F32), pltpu.VMEM((TOK, 1, HD), F32)],
        compiler_params=params(10),
        name="take_rows",
        cost_estimate=estimate(0, 8),
    )(index, back)
    all_heads = lax.all_to_all(
        taken.reshape(HEADS, HD, HD), ("hx", "hz"), 0, 0, tiled=True
    )
    whole = lambda *dims: pl.BlockSpec(dims, lambda n: (0,) * len(dims))
    w_specs = [
        pl.BlockSpec((depth, COLS), lambda n: (0, n)) for depth in (512, 512, 512, 256, 256)
    ]
    return pl.pallas_call(
        combine,
        grid=(WIDTH // 2 // COLS,),
        out_shape=shape((HD, WIDTH), BF),
        in_specs=[SMEM, whole(HEADS, HD, HD)] + w_specs * 2 + [whole(HD, WIDTH)],
        out_specs=whole(HD, WIDTH),
        scratch_shapes=[pltpu.VMEM((HD, WIDTH), BF)],
        compiler_params=params(16),
        name="combine",
        cost_estimate=estimate(2 * HD * WIDTH * WIDTH, 10),
    )(place, all_heads, *w_near, *w_far, own)


def solution(mesh):
    grid = Mesh(mesh.devices.reshape(SEQ, SIDE, SIDE), ("seq", "hx", "hz"))
    head = ("hx", "hz")
    in_specs = (
        P("seq", head),
        P(None, head),
        P(None, head),
        P(None, head),
        P(head, None),
        P("seq", head),
        P("seq", head),
    )
    out_specs = P(("seq", "hx", "hz"), None)
    return jax.shard_map(local, mesh=grid, in_specs=in_specs, out_specs=out_specs, check_vma=False)
```

```python
import math

import jax
import jax.numpy as jnp
from jax import lax
from jax.experimental import pallas as pl
from jax.experimental.pallas import tpu as pltpu
from jax.sharding import Mesh, PartitionSpec as P


HD = 128
BLOCK = 512
TOK = 2048
HALF = TOK // 2
SEQ = 8
SIDE = 4
HEADS = 16
WIDTH = 2048
BLK = 8
MOST = 64
ROWS = SEQ * BLK * MOST
MID = BLK // 2
TOLD = (BLK - MID + 1 + (BLK - MID) // 2) * MOST
SENT = TOLD + 16
REST = (MID - 1 + 1 + MID // 2) * MOST
LINE = 4
EMPTY = 1 << 20
POS = 1 << 14
OFFSETS = (0, -1, 1, 2)
SCALE = HD ** (-0.5) * math.log2(math.e)
BF = jnp.bfloat16
F32 = jnp.float32


VMEM = pl.BlockSpec(memory_space=pltpu.VMEM)
SMEM = pl.BlockSpec(memory_space=pltpu.SMEM)
HBM = pl.BlockSpec(memory_space=pltpu.HBM)


def params(mib):
    return pltpu.CompilerParams(vmem_limit_bytes=mib * 1024 * 1024)


def ring(by):
    return [(i, (i + by) % SIDE) for i in range(SIDE)]


def ring_gather(piece, axis):
    back = lax.ppermute(piece, axis, ring(1))
    ahead = lax.ppermute(piece, axis, ring(-1))
    half = piece.shape[0] // 2
    far_low = lax.ppermute(back[:half], axis, ring(1))
    far_high = lax.ppermute(ahead[half:], axis, ring(-1))
    return back, ahead, far_low, far_high


def gather_near(part, first, second):
    back, ahead, far_low, far_high = ring_gather(part, first)
    low = jnp.concatenate([part, back], 0)
    high = jnp.concatenate([ahead, far_low, far_high], 0)
    back_low = lax.ppermute(low, second, ring(1))
    ahead_low = lax.ppermute(low, second, ring(-1))
    ahead_high = lax.ppermute(high, second, ring(-1))
    back_high = lax.ppermute(high, second, ring(1))
    return low, high, back_low, back_high, ahead_low, ahead_high


def gather_far(near, second):
    return lax.ppermute(near[2], second, ring(1)), lax.ppermute(near[5], second, ring(-1))


def wrap(index, by):
    return lax.rem(index + (by + SIDE), SIDE)


def slice_of(place_ref, swapped, outer, inner):
    x, z = place_ref[0], place_ref[1]
    if swapped:
        return wrap(x, outer) * SIDE + wrap(z, inner)
    return wrap(x, inner) * SIDE + wrap(z, outer)


def piece_list(refs, outers):
    return [
        (refs[2 * n + m // 2], m % 2, outer, inner)
        for n, outer in enumerate(outers)
        for m, inner in enumerate(OFFSETS)
    ]


def fill_weights(place_ref, weights, target, swapped, outers):
    row = 0
    for outer in outers:
        for inner in OFFSETS:
            src = pl.multiple_of(slice_of(place_ref, swapped, outer, inner) * HD, HD)
            for n, w in enumerate(weights):
                target[row : row + HD, n * HD : (n + 1) * HD] = w[pl.ds(src, HD), :]
            row += HD


def pick_own(place_ref, halves, own_ref):
    head = place_ref[0] * SIDE + place_ref[1]
    per = HALF // HD
    for swapped, pieces in halves:
        row = head - per if swapped else head

        @pl.when((head >= per) if swapped else (head < per))
        def _():
            for ref, at, outer, inner in pieces:
                col = pl.multiple_of(slice_of(place_ref, swapped, outer, inner) * HD, HD)
                rows = pl.multiple_of(at * HALF + row * HD, HD)
                own_ref[:, pl.ds(col, HD)] = ref[pl.ds(rows, HD), :]


TILE = 256


def multiply(pieces, base, w, finish):
    def step(i, carry):
        lhs = jnp.concatenate(
            [
                ref[pl.ds(pl.multiple_of(at * HALF + i * TILE, TILE), TILE), :]
                for ref, at, _, _ in pieces
            ],
            1,
        )
        rows = pl.ds(pl.multiple_of(base + i * TILE, TILE), TILE)
        finish(rows, jnp.dot(lhs, w[...], preferred_element_type=F32))
        return carry

    lax.fori_loop(0, HALF // TILE, step, 0)


def project_near(place_ref, wq, wk, wv, *refs):
    acc_ref, own_ref, wa, wb = refs[12:]
    a, b = piece_list(refs[:6], OFFSETS[:3]), piece_list(refs[6:12], OFFSETS[:3])
    fill_weights(place_ref, (wq, wk, wv), wa, False, OFFSETS[:3])
    fill_weights(place_ref, (wq, wk, wv), wb, True, OFFSETS[:3])

    def finish(rows, total):
        acc_ref[rows, :] = total

    multiply(a, 0, wa, finish)
    multiply(b, HALF, wb, finish)
    pick_own(place_ref, ((False, a), (True, b)), own_ref)


def scatter_rows(index_ref, src, pad):
    def step(i, carry):
        for k in range(16):
            t = i * 16 + k
            pad[index_ref[t]] = src[t]
        return carry

    lax.fori_loop(0, TOK // 16, step, 0)


def project_far(place_ref, index_ref, wq, wk, wv, told, acc, own_in, a0, a1, b0, b1, *refs):
    out_ref, rest_refs, own_ref = refs[0], refs[1 : 1 + SEQ], refs[1 + SEQ]
    wa, wb, rows, pad, full, rest, sems, rest_sems = refs[2 + SEQ :]
    a, b = piece_list((a0, a1), OFFSETS[3:]), piece_list((b0, b1), OFFSETS[3:])
    fill_weights(place_ref, (wq, wk, wv), wa, False, OFFSETS[3:])
    fill_weights(place_ref, (wq, wk, wv), wb, True, OFFSETS[3:])

    def finish(at, total):
        total = (acc[at, :] + total).astype(BF).astype(F32)
        twice = pl.multiple_of(at.start * (ROWS // TOK), TILE)
        pad[pl.ds(twice, TILE * ROWS // TOK)] = jnp.zeros((TILE * ROWS // TOK, LINE, HD), F32)
        flat = rows.reshape(TOK * LINE, HD)
        start = pl.multiple_of(at.start * LINE, LINE)
        for k in range(3):
            flat[pl.ds(start + k, TILE, stride=LINE), :] = total[:, k * HD : (k + 1) * HD]

    multiply(a, 0, wa, finish)
    multiply(b, HALF, wb, finish)
    own_ref[...] = own_in[...]
    pick_own(place_ref, ((False, a), (True, b)), own_ref)
    scatter_rows(index_ref, rows, pad)
    flat = pad.reshape(ROWS * LINE, HD)

    def line(o, b, *kinds):
        at = (o * BLK + b) * MOST * LINE
        return jnp.concatenate(
            [flat[pl.ds(at + k, MOST, stride=LINE), :] for k in kinds], 1
        ).astype(BF)

    def put(target, o, n, value):
        target[o, n * MOST : (n + 1) * MOST, :] = value

    def queries(o, b):
        return jnp.concatenate([line(o, b, 0), line(o, b + 1, 0)], 1)

    def send(o):
        return pltpu.make_async_copy(full.at[o], out_ref.at[o], sems.at[o])

    def send_rest(d):
        o = lax.rem(place_ref[3] + d, SEQ)
        return pltpu.make_async_copy(rest.at[o], rest_refs[d], rest_sems.at[d])

    for o in range(SEQ):
        for n in range(MID - 1, BLK):
            put(full, o, n - (MID - 1), line(o, n, 1, 2))
        for n in range(MID, BLK, 2):
            put(full, o, BLK - MID + 1 + (n - MID) // 2, queries(o, n))
        full[o, TOLD:, :] = told[o]
        send(o).start()
    for o in range(SEQ):
        for n in range(MID - 1):
            put(rest, o, n, line(o, n, 1, 2))
        put(rest, o, MID - 1, line(o, -1, 1, 2) if o else jnp.zeros((MOST, 2 * HD), BF))
        for n in range(0, MID, 2):
            put(rest, o, MID + n // 2, queries(o, n))
    for d in range(SEQ):
        send_rest(d).start()
    for o in range(SEQ):
        send(o).wait()
    for d in range(SEQ):
        send_rest(d).wait()


def place_values(index_ref, value_ref, empty_ref, out_ref):
    pltpu.sync_copy(empty_ref, out_ref)

    def step(i, carry):
        for k in range(16):
            t = i * 16 + k
            out_ref[index_ref[t]] = value_ref[t]
        return carry

    lax.fori_loop(0, TOK // 16, step, 0)


QT = 128


def told_lines(got):
    digits = got[:, TOLD:, :].astype(F32)
    value = digits[:, 0:3] + digits[:, 3:6] * 256.0 + digits[:, 6:9] * 65536.0
    lines = []
    for b in range(-1, BLK):
        row, at = (2, 0) if b < 0 else (b // 4, b % 4 * MOST)
        lines.append(
            jnp.concatenate([value[s, row : row + 1, at : at + MOST] for s in range(SEQ)], 1)
        )
    return lines


def attend_blocks(blocks, lines, query_of, pair_of, scores, tops, full, send):
    column = jnp.concatenate(lines[1:], 0).T
    ones = jnp.ones((BLOCK, HD), BF)
    tiles = [(n, i) for n in range(len(blocks)) for i in range(BLOCK // QT)]

    def size(i):
        return QT // MOST * (i + 1), QT * (i + 1)

    def score(t):
        n, i = tiles[t]
        b = blocks[n]
        srcs, wide = size(i)
        base = jnp.floor(jnp.min(lines[b + 1], axis=1, keepdims=True) * (1.0 / POS)) * POS
        earlier = jnp.where(lines[b] >= base, lines[b], float(EMPTY))
        query = query_of(b, srcs)[i * QT :, :]
        mine = column[i * QT : (i + 1) * QT, b : b + 1]
        top = None
        for k, (which, line) in enumerate(((b - 1, earlier), (b, lines[b + 1]))):
            part = lax.dot_general(
                query,
                pair_of(which, srcs)[:, :HD],
                (((1,), (1,)), ((), ())),
                preferred_element_type=F32,
            )
            part = jnp.where(line[:, :wide] <= mine, part, F32(-1e30))
            scores[t % 2][:, k * wide : (k + 1) * wide] = part
            part = jnp.max(part, axis=1, keepdims=True)
            top = part if top is None else jnp.maximum(top, part)
        tops[t % 2][...] = jnp.broadcast_to(top, (QT, HD))

    def finish(t):
        n, i = tiles[t]
        b = blocks[n]
        srcs, wide = size(i)
        mixed = None
        for k, which in enumerate((b - 1, b)):
            top = jnp.concatenate([tops[t % 2][...]] * (wide // HD), 1)
            part = scores[t % 2][:, k * wide : (k + 1) * wide]
            expon = jnp.exp2((part - top) * F32(SCALE)).astype(BF)
            values = jnp.concatenate([pair_of(which, srcs)[:, HD:], ones[:wide]], 1)
            prod = jnp.dot(expon, values, preferred_element_type=F32)
            mixed = prod if mixed is None else mixed + prod
        done = (mixed[:, :HD] / mixed[:, HD:]).astype(BF)
        full[QT // MOST * i : srcs, n] = done.reshape(QT // MOST, MOST, HD)
        if i == BLOCK // QT - 1:
            send(n).start()

    score(0)
    for t in range(len(tiles)):
        if t + 1 < len(tiles):
            score(t + 1)
        finish(t)
    for n in range(len(blocks)):
        send(n).wait()


def rows_of(ref, n, srcs):
    return ref[:srcs, n * MOST : (n + 1) * MOST, :].reshape(srcs * MOST, 2 * HD)


def attend_late(got, out_ref, s0, s1, t0, t1, full, sems):
    def query_of(b, srcs):
        half = b % 2 * HD
        return rows_of(got, BLK - MID + 1 + (b - MID) // 2, srcs)[:, half : half + HD]

    def pair_of(b, srcs):
        return rows_of(got, b - (MID - 1), srcs)

    def send(n):
        return pltpu.make_async_copy(full.at[:, n], out_ref.at[:, n], sems.at[n])

    attend_blocks(
        range(MID, BLK), told_lines(got), query_of, pair_of, (s0, s1), (t0, t1), full, send
    )


def attend_early(place_ref, got, *refs):
    parts, out_ref = refs[:SEQ], refs[SEQ]
    rest, s0, s1, t0, t1, full, sems = refs[SEQ + 1 :]
    for d in range(SEQ):
        rest[lax.rem(place_ref[3] + (SEQ - d), SEQ)] = parts[d][...]

    def query_of(b, srcs):
        half = b % 2 * HD
        return rows_of(rest, MID + b // 2, srcs)[:, half : half + HD]

    def pair_of(b, srcs):
        if b == MID - 1:
            return rows_of(got, 0, srcs)
        return rows_of(rest, MID - 1 if b < 0 else b, srcs)

    def send(n):
        return pltpu.make_async_copy(full.at[:, n], out_ref.at[:, n], sems.at[n])

    attend_blocks(range(MID), told_lines(got), query_of, pair_of, (s0, s1), (t0, t1), full, send)


def take_rows(index_ref, early_ref, late_ref, out_ref, wide, taken):
    flat = wide.reshape(ROWS, HD)
    per = MID * MOST
    for o in range(SEQ):
        for n, ref in enumerate((early_ref, late_ref)):
            at = (2 * o + n) * per
            flat[at : at + per, :] = ref[o * per : (o + 1) * per, :].astype(F32)

    def step(i, carry):
        for k in range(16):
            t = i * 16 + k
            taken[t] = wide[index_ref[t]]
        return carry

    lax.fori_loop(0, TOK // 16, step, 0)
    out_ref[...] = taken.reshape(TOK, HD)[...].astype(BF)


COLS = 256


def combine(place_ref, rows_ref, *refs):
    near, far = refs[:5], refs[5:10]
    own_ref, out_ref, lhs = refs[10:]
    n = pl.program_id(0)

    @pl.when(n == 0)
    def _():
        for k, outer in enumerate(OFFSETS):
            for m, inner in enumerate(OFFSETS):
                h = slice_of(place_ref, False, outer, inner)
                col = (k * SIDE + m) * HD
                lhs[:, col : col + HD] = rows_ref[h]

    core = place_ref[2]
    for group, which in ((near, core), (far, 1 - core)):
        total, row = None, 0
        for w in group:
            depth = w.shape[0]
            prod = jnp.dot(lhs[:, row : row + depth], w[...], preferred_element_type=F32)
            total = prod if total is None else total + prod
            row += depth
        col = pl.ds(pl.multiple_of(which * (WIDTH // 2) + n * COLS, COLS), COLS)
        out_ref[:, col] = (total + own_ref[:, col].astype(F32)).astype(BF)


def estimate(flops, mib):
    return pl.CostEstimate(flops=flops, bytes_accessed=mib << 20, transcendentals=0)


def shape(dims, kind):
    return jax.ShapeDtypeStruct(dims, kind)


def sublayer(tokens, w_query, w_key, w_value, w_out, cluster_id, slot_index):
    x, z, seq = lax.axis_index("hx"), lax.axis_index("hz"), lax.axis_index("seq")
    core = lax.rem(seq, 2)
    place = jnp.stack([x, z, core, seq]).astype(jnp.int32)

    slots = slot_index.reshape(TOK)
    index = (slots // BLOCK) * MOST + slots % MOST
    value = cluster_id.reshape(TOK) * POS + seq * TOK + jnp.arange(TOK, dtype=jnp.int32)

    near_a = gather_near(tokens[:HALF], "hx", "hz")
    near_b = gather_near(tokens[HALF:], "hz", "hx")
    tied, _ = lax.optimization_barrier((index, near_b[5]))
    values = pl.pallas_call(
        place_values,
        out_shape=shape((ROWS,), jnp.int32),
        in_specs=[SMEM, SMEM, pl.BlockSpec(memory_space=pl.ANY)],
        out_specs=SMEM,
        name="place_values",
        cost_estimate=estimate(0, 12),
    )(tied, value, jnp.full((ROWS,), EMPTY, jnp.int32)).reshape(SEQ, BLK, MOST)
    halo = jnp.concatenate(
        [jnp.full((1, MOST), EMPTY, jnp.int32), values[: SEQ - 1, BLK - 1]], 0
    )
    halo = jnp.pad(halo, ((0, 0), (0, 2 * HD - MOST)))[:, None]
    values = jnp.concatenate([values.reshape(SEQ, 2, 2 * HD), halo], 1)
    told = jnp.concatenate([values & 255, (values >> 8) & 255, values >> 16], 1)
    told = jnp.pad(told, ((0, 0), (0, SENT - TOLD - 9), (0, 0))).astype(BF)

    weights = (w_query, w_key, w_value)
    acc, own = pl.pallas_call(
        project_near,
        out_shape=(shape((TOK, 3 * HD), F32), shape((HD, WIDTH), BF)),
        in_specs=[SMEM] + [VMEM] * 15,
        out_specs=(VMEM, VMEM),
        scratch_shapes=[pltpu.VMEM((12 * HD, 3 * HD), BF)] * 2,
        compiler_params=params(20),
        name="project_near",
        cost_estimate=estimate(2 * TOK * 12 * HD * 3 * HD, 10),
    )(place, *weights, *near_a, *near_b)
    far_a = gather_far(near_a, "hz")
    far_b = gather_far(near_b, "hx")
    sent, *rest, own = pl.pallas_call(
        project_far,
        out_shape=(
            pltpu.HBM((SEQ, SENT, 2 * HD), BF),
            *[pltpu.HBM((REST, 2 * HD), BF)] * SEQ,
            shape((HD, WIDTH), BF),
        ),
        in_specs=[SMEM, SMEM] + [VMEM] * 10,
        out_specs=(HBM,) * (1 + SEQ) + (VMEM,),
        scratch_shapes=[pltpu.VMEM((4 * HD, 3 * HD), BF)] * 2
        + [
            pltpu.VMEM((TOK, LINE, HD), F32),
            pltpu.VMEM((ROWS, LINE, HD), F32),
            pltpu.VMEM((SEQ, SENT, 2 * HD), BF),
            pltpu.VMEM((SEQ, REST, 2 * HD), BF),
            pltpu.SemaphoreType.DMA((SEQ,)),
            pltpu.SemaphoreType.DMA((SEQ,)),
        ],
        compiler_params=params(28),
        name="project_far",
        cost_estimate=estimate(2 * TOK * 4 * HD * 3 * HD, 24),
    )(place, index, *weights, told, acc, own, *far_a, *far_b)
    got = lax.all_to_all(sent, "seq", 0, 0, tiled=True)
    parts = [rest[0]]
    for d in range(1, SEQ):
        parts.append(lax.ppermute(rest[d], "seq", [(i, (i + d) % SEQ) for i in range(SEQ)]))

    w_half = lax.dynamic_slice_in_dim(w_out, core * (WIDTH // 2), WIDTH // 2, 1)
    w_half, _ = lax.optimization_barrier((w_half, own))
    w_row = jnp.concatenate((w_half,) + ring_gather(w_half, "hx"), 0)
    w_near = (w_row,) + ring_gather(w_row, "hz")
    w_far = tuple(lax.ppermute(w, "seq", [(i, i ^ 1) for i in range(SEQ)]) for w in w_near)

    scratch = [
        *[pltpu.VMEM((QT, 2 * BLOCK), F32)] * 2,
        *[pltpu.VMEM((QT, HD), F32)] * 2,
        pltpu.VMEM((SEQ, MID, MOST, HD), BF),
        pltpu.SemaphoreType.DMA((MID,)),
    ]
    late = pl.pallas_call(
        attend_late,
        out_shape=pltpu.HBM((SEQ, MID, MOST, HD), BF),
        in_specs=[VMEM],
        out_specs=HBM,
        scratch_shapes=scratch,
        compiler_params=params(12),
        name="attend_late",
        cost_estimate=estimate(4 * MID * BLOCK * 2 * BLOCK * HD, 6),
    )(got)
    late = lax.all_to_all(late, "seq", 0, 0, tiled=True).reshape(ROWS // 2, HD)
    early = pl.pallas_call(
        attend_early,
        out_shape=pltpu.HBM((SEQ, MID, MOST, HD), BF),
        in_specs=[SMEM] + [VMEM] * (1 + SEQ),
        out_specs=HBM,
        scratch_shapes=[pltpu.VMEM((SEQ, REST, 2 * HD), BF)] + scratch,
        compiler_params=params(16),
        name="attend_early",
        cost_estimate=estimate(4 * MID * BLOCK * 2 * BLOCK * HD, 8),
    )(place, got, *parts)
    early = lax.all_to_all(early, "seq", 0, 0, tiled=True).reshape(ROWS // 2, HD)
    taken = pl.pallas_call(
        take_rows,
        out_shape=shape((TOK, HD), BF),
        in_specs=[SMEM, VMEM, VMEM],
        out_specs=VMEM,
        scratch_shapes=[pltpu.VMEM((ROWS, 1, HD), F32), pltpu.VMEM((TOK, 1, HD), F32)],
        compiler_params=params(10),
        name="take_rows",
        cost_estimate=estimate(0, 8),
    )(index, early, late)
    all_heads = lax.all_to_all(
        taken.reshape(HEADS, HD, HD), ("hx", "hz"), 0, 0, tiled=True
    )
    whole = lambda *dims: pl.BlockSpec(dims, lambda n: (0,) * len(dims))
    w_specs = [
        pl.BlockSpec((depth, COLS), lambda n: (0, n)) for depth in (512, 512, 512, 256, 256)
    ]
    return pl.pallas_call(
        combine,
        grid=(WIDTH // 2 // COLS,),
        out_shape=shape((HD, WIDTH), BF),
        in_specs=[SMEM, whole(HEADS, HD, HD)] + w_specs * 2 + [whole(HD, WIDTH)],
        out_specs=whole(HD, WIDTH),
        scratch_shapes=[pltpu.VMEM((HD, WIDTH), BF)],
        compiler_params=params(16),
        name="combine",
        cost_estimate=estimate(2 * HD * WIDTH * WIDTH, 10),
    )(place, all_heads, *w_near, *w_far, own)


def solution(mesh):
    grid = Mesh(mesh.devices.reshape(SEQ, SIDE, SIDE), ("seq", "hx", "hz"))
    head = ("hx", "hz")
    in_specs = (
        P("seq", head),
        P(None, head),
        P(None, head),
        P(None, head),
        P(head, None),
        P("seq", head),
        P("seq", head),
    )
    out_specs = P(("seq", "hx", "hz"), None)
    return jax.shard_map(sublayer, mesh=grid, in_specs=in_specs, out_specs=out_specs, check_vma=False)
```

```python
import math

import jax
import jax.numpy as jnp
from jax import lax
from jax.experimental import pallas as pl
from jax.experimental.pallas import tpu as pltpu
from jax.sharding import Mesh, PartitionSpec as P


HD = 128
BLOCK = 512
TOK = 2048
HALF = TOK // 2
SEQ = 8
SIDE = 4
HEADS = 16
WIDTH = 2048
BLK = 8
MOST = 64
ROWS = SEQ * BLK * MOST
MID = BLK // 2
TOLD = (BLK - MID + 1 + (BLK - MID) // 2) * MOST
SENT = TOLD + 16
REST = (MID - 1 + 1 + MID // 2) * MOST
LINE = 4
EMPTY = 1 << 20
POS = 1 << 14
OFFSETS = (0, -1, 1, 2)
SCALE = HD ** (-0.5) * math.log2(math.e)
BF = jnp.bfloat16
F32 = jnp.float32


VMEM = pl.BlockSpec(memory_space=pltpu.VMEM)
SMEM = pl.BlockSpec(memory_space=pltpu.SMEM)
HBM = pl.BlockSpec(memory_space=pltpu.HBM)


def params(mib):
    return pltpu.CompilerParams(vmem_limit_bytes=mib * 1024 * 1024)


def ring(by):
    return [(i, (i + by) % SIDE) for i in range(SIDE)]


def shift(piece, axis, by):
    return lax.ppermute(piece, axis, ring(by))


def ring_gather(piece, axis):
    back = shift(piece, axis, 1)
    ahead = shift(piece, axis, -1)
    half = piece.shape[0] // 2
    far_low = shift(back[:half], axis, 1)
    far_high = shift(ahead[half:], axis, -1)
    return back, ahead, far_low, far_high


def gather_near(part, first, second):
    back, ahead, far_low, far_high = ring_gather(part, first)
    low = jnp.concatenate([part, back], 0)
    high = jnp.concatenate([ahead, far_low, far_high], 0)
    back_low = shift(low, second, 1)
    ahead_low = shift(low, second, -1)
    ahead_high = shift(high, second, -1)
    back_high = shift(high, second, 1)
    return low, high, back_low, back_high, ahead_low, ahead_high


def gather_far(near, second):
    return (shift(near[2], second, 1), shift(near[5], second, -1))


def wrap(index, by):
    return lax.rem(index + (by + SIDE), SIDE)


def slice_of(place_ref, swapped, outer, inner):
    x, z = place_ref[0], place_ref[1]
    if swapped:
        return wrap(x, outer) * SIDE + wrap(z, inner)
    return wrap(x, inner) * SIDE + wrap(z, outer)


def piece_list(refs, outers):
    return [
        (refs[2 * n + m // 2], m % 2, outer, inner)
        for n, outer in enumerate(outers)
        for m, inner in enumerate(OFFSETS)
    ]


def fill_weights(place_ref, weights, target, swapped, outers):
    row = 0
    for outer in outers:
        for inner in OFFSETS:
            src = pl.multiple_of(slice_of(place_ref, swapped, outer, inner) * HD, HD)
            for n, w in enumerate(weights):
                target[row : row + HD, n * HD : (n + 1) * HD] = w[pl.ds(src, HD), :]
            row += HD


def pick_own(place_ref, halves, own_ref):
    head = place_ref[0] * SIDE + place_ref[1]
    per = HALF // HD
    for swapped, pieces in halves:
        row = head - per if swapped else head

        @pl.when((head >= per) if swapped else (head < per))
        def _():
            for ref, at, outer, inner in pieces:
                col = pl.multiple_of(slice_of(place_ref, swapped, outer, inner) * HD, HD)
                rows = pl.multiple_of(at * HALF + row * HD, HD)
                own_ref[:, pl.ds(col, HD)] = ref[pl.ds(rows, HD), :]


TILE = 256


def multiply(pieces, base, w, finish):
    def step(i, carry):
        lhs = jnp.concatenate(
            [
                ref[pl.ds(pl.multiple_of(at * HALF + i * TILE, TILE), TILE), :]
                for ref, at, _, _ in pieces
            ],
            1,
        )
        rows = pl.ds(pl.multiple_of(base + i * TILE, TILE), TILE)
        finish(rows, jnp.dot(lhs, w[...], preferred_element_type=F32))
        return carry

    lax.fori_loop(0, HALF // TILE, step, 0)


def project_near(place_ref, wq, wk, wv, *refs):
    acc_ref, own_ref, wa, wb = refs[12:]
    a, b = piece_list(refs[:6], OFFSETS[:3]), piece_list(refs[6:12], OFFSETS[:3])
    fill_weights(place_ref, (wq, wk, wv), wa, False, OFFSETS[:3])
    fill_weights(place_ref, (wq, wk, wv), wb, True, OFFSETS[:3])

    def finish(rows, total):
        acc_ref[rows, :] = total

    multiply(a, 0, wa, finish)
    multiply(b, HALF, wb, finish)
    pick_own(place_ref, ((False, a), (True, b)), own_ref)


def scatter_rows(index_ref, src, pad):
    def step(i, carry):
        for k in range(16):
            t = i * 16 + k
            pad[index_ref[t]] = src[t]
        return carry

    lax.fori_loop(0, TOK // 16, step, 0)


def project_far(place_ref, index_ref, wq, wk, wv, told_ref, acc, own_in, a0, a1, b0, b1, *refs):
    out_ref, rest_refs, own_ref = refs[0], refs[1 : 1 + SEQ], refs[1 + SEQ]
    wa, wb, rows, pad, full, rest, sems, rest_sems = refs[2 + SEQ :]
    a, b = piece_list((a0, a1), OFFSETS[3:]), piece_list((b0, b1), OFFSETS[3:])
    fill_weights(place_ref, (wq, wk, wv), wa, False, OFFSETS[3:])
    fill_weights(place_ref, (wq, wk, wv), wb, True, OFFSETS[3:])

    def finish(at, total):
        total = (acc[at, :] + total).astype(BF).astype(F32)
        twice = pl.multiple_of(at.start * (ROWS // TOK), TILE)
        pad[pl.ds(twice, TILE * ROWS // TOK)] = jnp.zeros((TILE * ROWS // TOK, LINE, HD), F32)
        flat = rows.reshape(TOK * LINE, HD)
        start = pl.multiple_of(at.start * LINE, LINE)
        for k in range(3):
            flat[pl.ds(start + k, TILE, stride=LINE), :] = total[:, k * HD : (k + 1) * HD]
        flat[pl.ds(start + 3, TILE, stride=LINE), :] = told_ref[at, :]

    multiply(a, 0, wa, finish)
    multiply(b, HALF, wb, finish)
    own_ref[...] = own_in[...]
    pick_own(place_ref, ((False, a), (True, b)), own_ref)
    scatter_rows(index_ref, rows, pad)
    flat = pad.reshape(ROWS * LINE, HD)

    def line(o, b, *kinds):
        at = (o * BLK + b) * MOST * LINE
        return jnp.concatenate(
            [flat[pl.ds(at + k, MOST, stride=LINE), :] for k in kinds], 1
        ).astype(BF)

    def put(target, o, n, value):
        target[o, n * MOST : (n + 1) * MOST, :] = value

    def queries(o, b):
        return jnp.concatenate([line(o, b, 0), line(o, b + 1, 0)], 1)

    lane = lax.broadcasted_iota(jnp.int32, (MOST, HD), 1)
    slot = lax.broadcasted_iota(jnp.int32, (MOST, HD), 0)

    def told(o, b, shift):
        at = (o * BLK + b) * MOST * LINE + 3
        return jnp.where(lane == slot + shift, flat[pl.ds(at, MOST, stride=LINE), :], 0.0)

    def told_pair(o, b):
        return jnp.sum(told(o, b, 0) + told(o, b + 1, MOST), axis=0, keepdims=True)

    def digits(o):
        halo = told(o, -1, 0) if o else jnp.zeros((MOST, HD), F32)
        halo = jnp.sum(halo, axis=0, keepdims=True)
        values = [
            jnp.concatenate([told_pair(o, 0), told_pair(o, 2)], 1),
            jnp.concatenate([told_pair(o, 4), told_pair(o, 6)], 1),
            jnp.concatenate([halo, jnp.zeros_like(halo)], 1),
        ]
        high = [jnp.floor(v * (1.0 / 65536)) for v in values]
        left = [v - h * 65536.0 for v, h in zip(values, high)]
        middle = [jnp.floor(v * (1.0 / 256)) for v in left]
        low = [v - m * 256.0 for v, m in zip(left, middle)]
        unused = jnp.zeros((SENT - TOLD - 9, 2 * HD), F32)
        return jnp.concatenate(low + middle + high + [unused], 0).astype(BF)

    def send(o):
        return pltpu.make_async_copy(full.at[o], out_ref.at[o], sems.at[o])

    def send_rest(d):
        o = lax.rem(place_ref[3] + d, SEQ)
        return pltpu.make_async_copy(rest.at[o], rest_refs[d], rest_sems.at[d])

    for o in range(SEQ):
        for n in range(MID - 1, BLK):
            put(full, o, n - (MID - 1), line(o, n, 1, 2))
        for n in range(MID, BLK, 2):
            put(full, o, BLK - MID + 1 + (n - MID) // 2, queries(o, n))
        full[o, TOLD:, :] = digits(o)
        send(o).start()
    for o in range(SEQ):
        for n in range(MID - 1):
            put(rest, o, n, line(o, n, 1, 2))
        put(rest, o, MID - 1, line(o, -1, 1, 2) if o else jnp.zeros((MOST, 2 * HD), BF))
        for n in range(0, MID, 2):
            put(rest, o, MID + n // 2, queries(o, n))
    for d in range(SEQ):
        send_rest(d).start()
    for o in range(SEQ):
        send(o).wait()
    for d in range(SEQ):
        send_rest(d).wait()


QT = 128


def told_lines(got):
    digits = got[:, TOLD:, :].astype(F32)
    value = digits[:, 0:3] + digits[:, 3:6] * 256.0 + digits[:, 6:9] * 65536.0
    value = jnp.where(value > 0.0, value - 1.0, float(EMPTY))
    lines = []
    for b in range(-1, BLK):
        row, at = (2, 0) if b < 0 else (b // 4, b % 4 * MOST)
        lines.append(
            jnp.concatenate([value[s, row : row + 1, at : at + MOST] for s in range(SEQ)], 1)
        )
    return lines


def attend_blocks(blocks, lines, query_of, pair_of, scores, tops, full, send):
    column = jnp.concatenate(lines[1:], 0).T
    ones = jnp.ones((BLOCK, HD), BF)
    tiles = [(n, i) for n in range(len(blocks)) for i in range(BLOCK // QT)]

    def size(i):
        return QT // MOST * (i + 1), QT * (i + 1)

    def score(t):
        n, i = tiles[t]
        b = blocks[n]
        srcs, wide = size(i)
        base = jnp.floor(jnp.min(lines[b + 1], axis=1, keepdims=True) * (1.0 / POS)) * POS
        earlier = jnp.where(lines[b] >= base, lines[b], float(EMPTY))
        query = query_of(b, srcs)[i * QT :, :]
        mine = column[i * QT : (i + 1) * QT, b : b + 1]
        top = None
        for k, (which, line) in enumerate(((b - 1, earlier), (b, lines[b + 1]))):
            part = lax.dot_general(
                query,
                pair_of(which, srcs)[:, :HD],
                (((1,), (1,)), ((), ())),
                preferred_element_type=F32,
            )
            part = jnp.where(line[:, :wide] <= mine, part, F32(-1e30))
            scores[t % 2][:, k * wide : (k + 1) * wide] = part
            part = jnp.max(part, axis=1, keepdims=True)
            top = part if top is None else jnp.maximum(top, part)
        tops[t % 2][...] = jnp.broadcast_to(top, (QT, HD))

    def finish(t):
        n, i = tiles[t]
        b = blocks[n]
        srcs, wide = size(i)
        mixed = None
        for k, which in enumerate((b - 1, b)):
            top = jnp.concatenate([tops[t % 2][...]] * (wide // HD), 1)
            part = scores[t % 2][:, k * wide : (k + 1) * wide]
            expon = jnp.exp2((part - top) * F32(SCALE)).astype(BF)
            values = jnp.concatenate([pair_of(which, srcs)[:, HD:], ones[:wide]], 1)
            prod = jnp.dot(expon, values, preferred_element_type=F32)
            mixed = prod if mixed is None else mixed + prod
        done = (mixed[:, :HD] / mixed[:, HD:]).astype(BF)
        full[QT // MOST * i : srcs, n] = done.reshape(QT // MOST, MOST, HD)
        if i == BLOCK // QT - 1:
            send(n).start()

    score(0)
    for t in range(len(tiles)):
        if t + 1 < len(tiles):
            score(t + 1)
        finish(t)
    for n in range(len(blocks)):
        send(n).wait()


def rows_of(ref, n, srcs):
    return ref[:srcs, n * MOST : (n + 1) * MOST, :].reshape(srcs * MOST, 2 * HD)


def attend_late(got, out_ref, s0, s1, t0, t1, full, sems):
    def query_of(b, srcs):
        half = b % 2 * HD
        return rows_of(got, BLK - MID + 1 + (b - MID) // 2, srcs)[:, half : half + HD]

    def pair_of(b, srcs):
        return rows_of(got, b - (MID - 1), srcs)

    def send(n):
        return pltpu.make_async_copy(full.at[:, n], out_ref.at[:, n], sems.at[n])

    attend_blocks(
        range(MID, BLK), told_lines(got), query_of, pair_of, (s0, s1), (t0, t1), full, send
    )


def attend_early(place_ref, got, *refs):
    parts, out_ref = refs[:SEQ], refs[SEQ]
    rest, s0, s1, t0, t1, full, sems = refs[SEQ + 1 :]
    for d in range(SEQ):
        rest[lax.rem(place_ref[3] + (SEQ - d), SEQ)] = parts[d][...]

    def query_of(b, srcs):
        half = b % 2 * HD
        return rows_of(rest, MID + b // 2, srcs)[:, half : half + HD]

    def pair_of(b, srcs):
        if b == MID - 1:
            return rows_of(got, 0, srcs)
        return rows_of(rest, MID - 1 if b < 0 else b, srcs)

    def send(n):
        return pltpu.make_async_copy(full.at[:, n], out_ref.at[:, n], sems.at[n])

    attend_blocks(range(MID), told_lines(got), query_of, pair_of, (s0, s1), (t0, t1), full, send)


def take_rows(index_ref, early_ref, late_ref, out_ref, wide, taken):
    flat = wide.reshape(ROWS, HD)
    per = MID * MOST
    for o in range(SEQ):
        for n, ref in enumerate((early_ref, late_ref)):
            at = (2 * o + n) * per
            flat[at : at + per, :] = ref[o * per : (o + 1) * per, :].astype(F32)

    def step(i, carry):
        for k in range(16):
            t = i * 16 + k
            taken[t] = wide[index_ref[t]]
        return carry

    lax.fori_loop(0, TOK // 16, step, 0)
    out_ref[...] = taken.reshape(TOK, HD)[...].astype(BF)


COLS = 256


def combine(place_ref, rows_ref, *refs):
    near, far = refs[:5], refs[5:10]
    own_ref, out_ref, lhs = refs[10:]
    n = pl.program_id(0)

    @pl.when(n == 0)
    def _():
        for k, outer in enumerate(OFFSETS):
            for m, inner in enumerate(OFFSETS):
                h = slice_of(place_ref, False, outer, inner)
                col = (k * SIDE + m) * HD
                lhs[:, col : col + HD] = rows_ref[h]

    core = place_ref[2]
    for group, which in ((near, core), (far, 1 - core)):
        total, row = None, 0
        for w in group:
            depth = w.shape[0]
            prod = jnp.dot(lhs[:, row : row + depth], w[...], preferred_element_type=F32)
            total = prod if total is None else total + prod
            row += depth
        col = pl.ds(pl.multiple_of(which * (WIDTH // 2) + n * COLS, COLS), COLS)
        out_ref[:, col] = (total + own_ref[:, col].astype(F32)).astype(BF)


def estimate(flops, mib):
    return pl.CostEstimate(flops=flops, bytes_accessed=mib << 20, transcendentals=0)


def shape(dims, kind):
    return jax.ShapeDtypeStruct(dims, kind)


def sublayer(tokens, w_query, w_key, w_value, w_out, cluster_id, slot_index):
    x, z, seq = lax.axis_index("hx"), lax.axis_index("hz"), lax.axis_index("seq")
    core = lax.rem(seq, 2)
    place = jnp.stack([x, z, core, seq]).astype(jnp.int32)

    slots = slot_index.reshape(TOK)
    index = (slots // BLOCK) * MOST + slots % MOST
    value = cluster_id * POS + 1 + seq * TOK + lax.broadcasted_iota(jnp.int32, (TOK, 1), 0)
    told = jnp.broadcast_to(value.astype(F32), (TOK, HD))

    near_a = gather_near(tokens[:HALF], "hx", "hz")
    near_b = gather_near(tokens[HALF:], "hz", "hx")
    w_half = lax.dynamic_slice_in_dim(w_out, core * (WIDTH // 2), WIDTH // 2, 1)
    w_row = (w_half,) + ring_gather(w_half, "hx")

    weights = (w_query, w_key, w_value)
    acc, own = pl.pallas_call(
        project_near,
        out_shape=(shape((TOK, 3 * HD), F32), shape((HD, WIDTH), BF)),
        in_specs=[SMEM] + [VMEM] * 15,
        out_specs=(VMEM, VMEM),
        scratch_shapes=[pltpu.VMEM((12 * HD, 3 * HD), BF)] * 2,
        compiler_params=params(20),
        name="project_near",
        cost_estimate=estimate(2 * TOK * 12 * HD * 3 * HD, 10),
    )(place, *weights, *near_a, *near_b)
    far_a = gather_far(near_a, "hz")
    far_b = gather_far(near_b, "hx")
    sent, *rest, own = pl.pallas_call(
        project_far,
        out_shape=(
            pltpu.HBM((SEQ, SENT, 2 * HD), BF),
            *[pltpu.HBM((REST, 2 * HD), BF)] * SEQ,
            shape((HD, WIDTH), BF),
        ),
        in_specs=[SMEM, SMEM] + [VMEM] * 10,
        out_specs=(HBM,) * (1 + SEQ) + (VMEM,),
        scratch_shapes=[pltpu.VMEM((4 * HD, 3 * HD), BF)] * 2
        + [
            pltpu.VMEM((TOK, LINE, HD), F32),
            pltpu.VMEM((ROWS, LINE, HD), F32),
            pltpu.VMEM((SEQ, SENT, 2 * HD), BF),
            pltpu.VMEM((SEQ, REST, 2 * HD), BF),
            pltpu.SemaphoreType.DMA((SEQ,)),
            pltpu.SemaphoreType.DMA((SEQ,)),
        ],
        compiler_params=params(28),
        name="project_far",
        cost_estimate=estimate(2 * TOK * 4 * HD * 3 * HD, 24),
    )(place, index, *weights, told, acc, own, *far_a, *far_b)
    got = lax.all_to_all(sent, "seq", 0, 0, tiled=True)
    parts = [rest[0]]
    for d in range(1, SEQ):
        parts.append(lax.ppermute(rest[d], "seq", [(i, (i + d) % SEQ) for i in range(SEQ)]))

    w_row, _ = lax.optimization_barrier((w_row, own))
    w_row = jnp.concatenate(w_row, 0)
    w_near = (w_row,) + ring_gather(w_row, "hz")
    w_far = tuple(lax.ppermute(w, "seq", [(i, i ^ 1) for i in range(SEQ)]) for w in w_near)

    scratch = [
        *[pltpu.VMEM((QT, 2 * BLOCK), F32)] * 2,
        *[pltpu.VMEM((QT, HD), F32)] * 2,
        pltpu.VMEM((SEQ, MID, MOST, HD), BF),
        pltpu.SemaphoreType.DMA((MID,)),
    ]
    late = pl.pallas_call(
        attend_late,
        out_shape=pltpu.HBM((SEQ, MID, MOST, HD), BF),
        in_specs=[VMEM],
        out_specs=HBM,
        scratch_shapes=scratch,
        compiler_params=params(12),
        name="attend_late",
        cost_estimate=estimate(4 * MID * BLOCK * 2 * BLOCK * HD, 6),
    )(got)
    late = lax.all_to_all(late, "seq", 0, 0, tiled=True).reshape(ROWS // 2, HD)
    early = pl.pallas_call(
        attend_early,
        out_shape=pltpu.HBM((SEQ, MID, MOST, HD), BF),
        in_specs=[SMEM] + [VMEM] * (1 + SEQ),
        out_specs=HBM,
        scratch_shapes=[pltpu.VMEM((SEQ, REST, 2 * HD), BF)] + scratch,
        compiler_params=params(16),
        name="attend_early",
        cost_estimate=estimate(4 * MID * BLOCK * 2 * BLOCK * HD, 8),
    )(place, got, *parts)
    early = lax.all_to_all(early, "seq", 0, 0, tiled=True).reshape(ROWS // 2, HD)
    taken = pl.pallas_call(
        take_rows,
        out_shape=shape((TOK, HD), BF),
        in_specs=[SMEM, VMEM, VMEM],
        out_specs=VMEM,
        scratch_shapes=[pltpu.VMEM((ROWS, 1, HD), F32), pltpu.VMEM((TOK, 1, HD), F32)],
        compiler_params=params(10),
        name="take_rows",
        cost_estimate=estimate(0, 8),
    )(index, early, late)
    all_heads = lax.all_to_all(
        taken.reshape(HEADS, HD, HD), ("hx", "hz"), 0, 0, tiled=True
    )
    whole = lambda *dims: pl.BlockSpec(dims, lambda n: (0,) * len(dims))
    w_specs = [
        pl.BlockSpec((depth, COLS), lambda n: (0, n)) for depth in (512, 512, 512, 256, 256)
    ]
    return pl.pallas_call(
        combine,
        grid=(WIDTH // 2 // COLS,),
        out_shape=shape((HD, WIDTH), BF),
        in_specs=[SMEM, whole(HEADS, HD, HD)] + w_specs * 2 + [whole(HD, WIDTH)],
        out_specs=whole(HD, WIDTH),
        scratch_shapes=[pltpu.VMEM((HD, WIDTH), BF)],
        compiler_params=params(16),
        name="combine",
        cost_estimate=estimate(2 * HD * WIDTH * WIDTH, 10),
    )(place, all_heads, *w_near, *w_far, own)


def solution(mesh):
    grid = Mesh(mesh.devices.reshape(SEQ, SIDE, SIDE), ("seq", "hx", "hz"))
    head = ("hx", "hz")
    in_specs = (
        P("seq", head),
        P(None, head),
        P(None, head),
        P(None, head),
        P(head, None),
        P("seq", head),
        P("seq", head),
    )
    out_specs = P(("seq", "hx", "hz"), None)
    return jax.shard_map(sublayer, mesh=grid, in_specs=in_specs, out_specs=out_specs, check_vma=False)
```

```python
import math

import jax
import jax.numpy as jnp
from jax import lax
from jax.experimental import pallas as pl
from jax.experimental.pallas import tpu as pltpu
from jax.sharding import Mesh, PartitionSpec as P


HD = 128
BLOCK = 512
TOK = 2048
HALF = TOK // 2
SEQ = 8
SIDE = 4
HEADS = 16
WIDTH = 2048
BLK = 8
MOST = 64
ROWS = SEQ * BLK * MOST
MID = BLK // 2
TOLD = (BLK - MID + 1 + (BLK - MID) // 2) * MOST
SENT = TOLD + 16
REST = (MID - 1 + 1 + MID // 2) * MOST
LINE = 4
EMPTY = 1 << 20
POS = 1 << 14
OFFSETS = (0, -1, 1, 2)
SCALE = HD ** (-0.5) * math.log2(math.e)
BF = jnp.bfloat16
F32 = jnp.float32


VMEM = pl.BlockSpec(memory_space=pltpu.VMEM)
SMEM = pl.BlockSpec(memory_space=pltpu.SMEM)
HBM = pl.BlockSpec(memory_space=pltpu.HBM)


def params(mib):
    return pltpu.CompilerParams(vmem_limit_bytes=mib * 1024 * 1024)


def ring(by):
    return [(i, (i + by) % SIDE) for i in range(SIDE)]


def shift(piece, axis, by):
    return lax.ppermute(piece, axis, ring(by))


def ring_gather(piece, axis):
    back = shift(piece, axis, 1)
    ahead = shift(piece, axis, -1)
    half = piece.shape[0] // 2
    far_low = shift(back[:half], axis, 1)
    far_high = shift(ahead[half:], axis, -1)
    return back, ahead, far_low, far_high


def gather_near(part, first, second):
    back, ahead, far_low, far_high = ring_gather(part, first)
    low = jnp.concatenate([part, back], 0)
    high = jnp.concatenate([ahead, far_low, far_high], 0)
    back_low = shift(low, second, 1)
    ahead_low = shift(low, second, -1)
    ahead_high = shift(high, second, -1)
    back_high = shift(high, second, 1)
    return low, high, back_low, back_high, ahead_low, ahead_high


def gather_far(near, second):
    return (shift(near[2], second, 1), shift(near[5], second, -1))


def wrap(index, by):
    return lax.rem(index + (by + SIDE), SIDE)


def slice_of(place_ref, swapped, outer, inner):
    x, z = place_ref[0], place_ref[1]
    if swapped:
        return wrap(x, outer) * SIDE + wrap(z, inner)
    return wrap(x, inner) * SIDE + wrap(z, outer)


def piece_list(refs, outers):
    return [
        (refs[2 * n + m // 2], m % 2, outer, inner)
        for n, outer in enumerate(outers)
        for m, inner in enumerate(OFFSETS)
    ]


def fill_weights(place_ref, weights, target, swapped, outers):
    row = 0
    for outer in outers:
        for inner in OFFSETS:
            src = pl.multiple_of(slice_of(place_ref, swapped, outer, inner) * HD, HD)
            for n, w in enumerate(weights):
                target[row : row + HD, n * HD : (n + 1) * HD] = w[pl.ds(src, HD), :]
            row += HD


def pick_own(place_ref, halves, own_ref):
    head = place_ref[0] * SIDE + place_ref[1]
    per = HALF // HD
    for swapped, pieces in halves:
        row = head - per if swapped else head

        @pl.when((head >= per) if swapped else (head < per))
        def _():
            for ref, at, outer, inner in pieces:
                col = pl.multiple_of(slice_of(place_ref, swapped, outer, inner) * HD, HD)
                rows = pl.multiple_of(at * HALF + row * HD, HD)
                own_ref[:, pl.ds(col, HD)] = ref[pl.ds(rows, HD), :]


TILE = 256


def multiply(pieces, base, w, finish):
    def step(i, carry):
        lhs = jnp.concatenate(
            [
                ref[pl.ds(pl.multiple_of(at * HALF + i * TILE, TILE), TILE), :]
                for ref, at, _, _ in pieces
            ],
            1,
        )
        rows = pl.ds(pl.multiple_of(base + i * TILE, TILE), TILE)
        finish(rows, jnp.dot(lhs, w[...], preferred_element_type=F32))
        return carry

    lax.fori_loop(0, HALF // TILE, step, 0)


def project_near(place_ref, wq, wk, wv, *refs):
    acc_ref, own_ref, wa, wb = refs[12:]
    a, b = piece_list(refs[:6], OFFSETS[:3]), piece_list(refs[6:12], OFFSETS[:3])
    fill_weights(place_ref, (wq, wk, wv), wa, False, OFFSETS[:3])
    fill_weights(place_ref, (wq, wk, wv), wb, True, OFFSETS[:3])

    def finish(rows, total):
        acc_ref[rows, :] = total

    multiply(a, 0, wa, finish)
    multiply(b, HALF, wb, finish)
    pick_own(place_ref, ((False, a), (True, b)), own_ref)


def scatter_rows(index_ref, src, pad):
    def step(i, carry):
        for k in range(16):
            t = i * 16 + k
            pad[index_ref[t]] = src[t]
        return carry

    lax.fori_loop(0, TOK // 16, step, 0)


def project_far(place_ref, index_ref, wq, wk, wv, told_ref, acc, own_in, a0, a1, b0, b1, *refs):
    out_ref, rest_refs, own_ref = refs[0], refs[1 : 1 + SEQ], refs[1 + SEQ]
    wa, wb, rows, pad, full, rest, sems, rest_sems = refs[2 + SEQ :]
    a, b = piece_list((a0, a1), OFFSETS[3:]), piece_list((b0, b1), OFFSETS[3:])
    fill_weights(place_ref, (wq, wk, wv), wa, False, OFFSETS[3:])
    fill_weights(place_ref, (wq, wk, wv), wb, True, OFFSETS[3:])

    def finish(at, total):
        total = (acc[at, :] + total).astype(BF).astype(F32)
        twice = pl.multiple_of(at.start * (ROWS // TOK), TILE)
        pad[pl.ds(twice, TILE * ROWS // TOK)] = jnp.zeros((TILE * ROWS // TOK, LINE, HD), F32)
        flat = rows.reshape(TOK * LINE, HD)
        start = pl.multiple_of(at.start * LINE, LINE)
        for k in range(3):
            flat[pl.ds(start + k, TILE, stride=LINE), :] = total[:, k * HD : (k + 1) * HD]
        flat[pl.ds(start + 3, TILE, stride=LINE), :] = told_ref[at, :]

    multiply(a, 0, wa, finish)
    multiply(b, HALF, wb, finish)
    own_ref[...] = own_in[...]
    pick_own(place_ref, ((False, a), (True, b)), own_ref)
    scatter_rows(index_ref, rows, pad)
    flat = pad.reshape(ROWS * LINE, HD)

    def line(o, b, *kinds):
        at = (o * BLK + b) * MOST * LINE
        return jnp.concatenate(
            [flat[pl.ds(at + k, MOST, stride=LINE), :] for k in kinds], 1
        ).astype(BF)

    def put(target, o, n, value):
        target[o, n * MOST : (n + 1) * MOST, :] = value

    def queries(o, b):
        return jnp.concatenate([line(o, b, 0), line(o, b + 1, 0)], 1)

    lane = lax.broadcasted_iota(jnp.int32, (MOST, HD), 1)
    slot = lax.broadcasted_iota(jnp.int32, (MOST, HD), 0)

    def told(o, b, shift):
        at = (o * BLK + b) * MOST * LINE + 3
        return jnp.where(lane == slot + shift, flat[pl.ds(at, MOST, stride=LINE), :], 0.0)

    def told_pair(o, b):
        return jnp.sum(told(o, b, 0) + told(o, b + 1, MOST), axis=0, keepdims=True)

    def digits(o):
        halo = told(o, -1, 0) if o else jnp.zeros((MOST, HD), F32)
        halo = jnp.sum(halo, axis=0, keepdims=True)
        values = [
            jnp.concatenate([told_pair(o, 0), told_pair(o, 2)], 1),
            jnp.concatenate([told_pair(o, 4), told_pair(o, 6)], 1),
            jnp.concatenate([halo, jnp.zeros_like(halo)], 1),
        ]
        high = [jnp.floor(v * (1.0 / 65536)) for v in values]
        left = [v - h * 65536.0 for v, h in zip(values, high)]
        middle = [jnp.floor(v * (1.0 / 256)) for v in left]
        low = [v - m * 256.0 for v, m in zip(left, middle)]
        unused = jnp.zeros((SENT - TOLD - 9, 2 * HD), F32)
        return jnp.concatenate(low + middle + high + [unused], 0).astype(BF)

    def send(o):
        return pltpu.make_async_copy(full.at[o], out_ref.at[o], sems.at[o])

    def send_rest(d):
        o = lax.rem(place_ref[3] + d, SEQ)
        return pltpu.make_async_copy(rest.at[o], rest_refs[d], rest_sems.at[d])

    for o in range(SEQ):
        for n in range(MID - 1, BLK):
            put(full, o, n - (MID - 1), line(o, n, 1, 2))
        for n in range(MID, BLK, 2):
            put(full, o, BLK - MID + 1 + (n - MID) // 2, queries(o, n))
        full[o, TOLD:, :] = digits(o)
        send(o).start()
    for o in range(SEQ):
        for n in range(MID - 1):
            put(rest, o, n, line(o, n, 1, 2))
        put(rest, o, MID - 1, line(o, -1, 1, 2) if o else jnp.zeros((MOST, 2 * HD), BF))
        for n in range(0, MID, 2):
            put(rest, o, MID + n // 2, queries(o, n))
    for d in range(SEQ):
        send_rest(d).start()
    for o in range(SEQ):
        send(o).wait()
    for d in range(SEQ):
        send_rest(d).wait()


QT = 128


def told_lines(got):
    digits = got[:, TOLD:, :].astype(F32)
    value = digits[:, 0:3] + digits[:, 3:6] * 256.0 + digits[:, 6:9] * 65536.0
    value = jnp.where(value > 0.0, value - 1.0, float(EMPTY))
    lines = []
    for b in range(-1, BLK):
        row, at = (2, 0) if b < 0 else (b // 4, b % 4 * MOST)
        lines.append(
            jnp.concatenate([value[s, row : row + 1, at : at + MOST] for s in range(SEQ)], 1)
        )
    return lines


def attend_blocks(blocks, lines, query_of, pair_of, scores, tops, full, send):
    column = jnp.concatenate(lines[1:], 0).T
    ones = jnp.ones((BLOCK, HD), BF)
    tiles = [(n, i) for n in range(len(blocks)) for i in range(BLOCK // QT)]

    def size(i):
        return QT // MOST * (i + 1), QT * (i + 1)

    def score(t):
        n, i = tiles[t]
        b = blocks[n]
        srcs, wide = size(i)
        base = jnp.floor(jnp.min(lines[b + 1], axis=1, keepdims=True) * (1.0 / POS)) * POS
        earlier = jnp.where(lines[b] >= base, lines[b], float(EMPTY))
        query = query_of(b, srcs)[i * QT :, :]
        mine = column[i * QT : (i + 1) * QT, b : b + 1]
        top = None
        for k, (which, line) in enumerate(((b - 1, earlier), (b, lines[b + 1]))):
            part = lax.dot_general(
                query,
                pair_of(which, srcs)[:, :HD],
                (((1,), (1,)), ((), ())),
                preferred_element_type=F32,
            )
            part = jnp.where(line[:, :wide] <= mine, part, F32(-1e30))
            scores[t % 2][:, k * wide : (k + 1) * wide] = part
            part = jnp.max(part, axis=1, keepdims=True)
            top = part if top is None else jnp.maximum(top, part)
        tops[t % 2][...] = jnp.broadcast_to(top, (QT, HD))

    def finish(t):
        n, i = tiles[t]
        b = blocks[n]
        srcs, wide = size(i)
        mixed = None
        for k, which in enumerate((b - 1, b)):
            top = jnp.concatenate([tops[t % 2][...]] * (wide // HD), 1)
            part = scores[t % 2][:, k * wide : (k + 1) * wide]
            expon = jnp.exp2((part - top) * F32(SCALE)).astype(BF)
            values = jnp.concatenate([pair_of(which, srcs)[:, HD:], ones[:wide]], 1)
            prod = jnp.dot(expon, values, preferred_element_type=F32)
            mixed = prod if mixed is None else mixed + prod
        done = (mixed[:, :HD] / mixed[:, HD:]).astype(BF)
        full[QT // MOST * i : srcs, n] = done.reshape(QT // MOST, MOST, HD)
        if i == BLOCK // QT - 1:
            send(n).start()

    score(0)
    for t in range(len(tiles)):
        if t + 1 < len(tiles):
            score(t + 1)
        finish(t)
    for n in range(len(blocks)):
        send(n).wait()


def rows_of(ref, n, srcs):
    return ref[:srcs, n * MOST : (n + 1) * MOST, :].reshape(srcs * MOST, 2 * HD)


def attend_late(got, out_ref, s0, s1, t0, t1, full, sems):
    def query_of(b, srcs):
        half = b % 2 * HD
        return rows_of(got, BLK - MID + 1 + (b - MID) // 2, srcs)[:, half : half + HD]

    def pair_of(b, srcs):
        return rows_of(got, b - (MID - 1), srcs)

    def send(n):
        return pltpu.make_async_copy(full.at[:, n], out_ref.at[:, n], sems.at[n])

    attend_blocks(
        range(MID, BLK), told_lines(got), query_of, pair_of, (s0, s1), (t0, t1), full, send
    )


def attend_early(place_ref, got, *refs):
    parts, out_ref = refs[:SEQ], refs[SEQ]
    rest, s0, s1, t0, t1, full, sems = refs[SEQ + 1 :]
    for d in range(SEQ):
        rest[lax.rem(place_ref[3] + (SEQ - d), SEQ)] = parts[d][...]

    def query_of(b, srcs):
        half = b % 2 * HD
        return rows_of(rest, MID + b // 2, srcs)[:, half : half + HD]

    def pair_of(b, srcs):
        if b == MID - 1:
            return rows_of(got, 0, srcs)
        return rows_of(rest, MID - 1 if b < 0 else b, srcs)

    def send(n):
        return pltpu.make_async_copy(full.at[:, n], out_ref.at[:, n], sems.at[n])

    attend_blocks(range(MID), told_lines(got), query_of, pair_of, (s0, s1), (t0, t1), full, send)


def take_rows(index_ref, early_ref, late_ref, out_ref, wide, taken):
    flat = wide.reshape(ROWS, HD)
    per = MID * MOST
    for o in range(SEQ):
        for n, ref in enumerate((early_ref, late_ref)):
            at = (2 * o + n) * per
            flat[at : at + per, :] = ref[o * per : (o + 1) * per, :].astype(F32)

    def step(i, carry):
        for k in range(16):
            t = i * 16 + k
            taken[t] = wide[index_ref[t]]
        return carry

    lax.fori_loop(0, TOK // 16, step, 0)
    out_ref[...] = taken.reshape(TOK, HD)[...].astype(BF)


COLS = 256


def combine(place_ref, rows_ref, *refs):
    near, far = refs[:5], refs[5:10]
    own_ref, out_ref, lhs = refs[10:]
    n = pl.program_id(0)

    @pl.when(n == 0)
    def _():
        for k, outer in enumerate(OFFSETS):
            for m, inner in enumerate(OFFSETS):
                h = slice_of(place_ref, False, outer, inner)
                col = (k * SIDE + m) * HD
                lhs[:, col : col + HD] = rows_ref[h]

    core = place_ref[2]
    for group, which in ((near, core), (far, 1 - core)):
        total, row = None, 0
        for w in group:
            depth = w.shape[0]
            prod = jnp.dot(lhs[:, row : row + depth], w[...], preferred_element_type=F32)
            total = prod if total is None else total + prod
            row += depth
        col = pl.ds(pl.multiple_of(which * (WIDTH // 2) + n * COLS, COLS), COLS)
        out_ref[:, col] = (total + own_ref[:, col].astype(F32)).astype(BF)


def estimate(flops, mib):
    return pl.CostEstimate(flops=flops, bytes_accessed=mib << 20, transcendentals=0)


def shape(dims, kind):
    return jax.ShapeDtypeStruct(dims, kind)


def sublayer(tokens, w_query, w_key, w_value, w_out, cluster_id, slot_index):
    x, z, seq = lax.axis_index("hx"), lax.axis_index("hz"), lax.axis_index("seq")
    core = lax.rem(seq, 2)
    place = jnp.stack([x, z, core, seq]).astype(jnp.int32)

    slots = slot_index.reshape(TOK)
    index = (slots // BLOCK) * MOST + slots % MOST
    value = cluster_id * POS + 1 + seq * TOK + lax.broadcasted_iota(jnp.int32, (TOK, 1), 0)
    told = jnp.broadcast_to(value.astype(F32), (TOK, HD))

    near_a = gather_near(tokens[:HALF], "hx", "hz")
    near_b = gather_near(tokens[HALF:], "hz", "hx")
    w_half = lax.dynamic_slice_in_dim(w_out, core * (WIDTH // 2), WIDTH // 2, 1)
    w_row = (w_half,) + tuple(shift(w_half, "hx", -by) for by in OFFSETS[1:])

    weights = (w_query, w_key, w_value)
    acc, own = pl.pallas_call(
        project_near,
        out_shape=(shape((TOK, 3 * HD), F32), shape((HD, WIDTH), BF)),
        in_specs=[SMEM] + [VMEM] * 15,
        out_specs=(VMEM, VMEM),
        scratch_shapes=[pltpu.VMEM((12 * HD, 3 * HD), BF)] * 2,
        compiler_params=params(20),
        name="project_near",
        cost_estimate=estimate(2 * TOK * 12 * HD * 3 * HD, 10),
    )(place, *weights, *near_a, *near_b)
    far_a = gather_far(near_a, "hz")
    far_b = gather_far(near_b, "hx")
    sent, *rest, own = pl.pallas_call(
        project_far,
        out_shape=(
            pltpu.HBM((SEQ, SENT, 2 * HD), BF),
            *[pltpu.HBM((REST, 2 * HD), BF)] * SEQ,
            shape((HD, WIDTH), BF),
        ),
        in_specs=[SMEM, SMEM] + [VMEM] * 10,
        out_specs=(HBM,) * (1 + SEQ) + (VMEM,),
        scratch_shapes=[pltpu.VMEM((4 * HD, 3 * HD), BF)] * 2
        + [
            pltpu.VMEM((TOK, LINE, HD), F32),
            pltpu.VMEM((ROWS, LINE, HD), F32),
            pltpu.VMEM((SEQ, SENT, 2 * HD), BF),
            pltpu.VMEM((SEQ, REST, 2 * HD), BF),
            pltpu.SemaphoreType.DMA((SEQ,)),
            pltpu.SemaphoreType.DMA((SEQ,)),
        ],
        compiler_params=params(28),
        name="project_far",
        cost_estimate=estimate(2 * TOK * 4 * HD * 3 * HD, 24),
    )(place, index, *weights, told, acc, own, *far_a, *far_b)
    got = lax.all_to_all(sent, "seq", 0, 0, tiled=True)
    parts = [rest[0]]
    for d in range(1, SEQ):
        parts.append(lax.ppermute(rest[d], "seq", [(i, (i + d) % SEQ) for i in range(SEQ)]))

    w_row, _ = lax.optimization_barrier((w_row, own))
    w_row = jnp.concatenate(w_row, 0)
    w_near = (w_row,) + ring_gather(w_row, "hz")
    w_far = []
    for w in w_near:
        w_far.append(lax.ppermute(w, "seq", [(i, i ^ 1) for i in range(SEQ)]))

    scratch = [
        *[pltpu.VMEM((QT, 2 * BLOCK), F32)] * 2,
        *[pltpu.VMEM((QT, HD), F32)] * 2,
        pltpu.VMEM((SEQ, MID, MOST, HD), BF),
        pltpu.SemaphoreType.DMA((MID,)),
    ]
    late = pl.pallas_call(
        attend_late,
        out_shape=pltpu.HBM((SEQ, MID, MOST, HD), BF),
        in_specs=[VMEM],
        out_specs=HBM,
        scratch_shapes=scratch,
        compiler_params=params(12),
        name="attend_late",
        cost_estimate=estimate(4 * MID * BLOCK * 2 * BLOCK * HD, 6),
    )(got)
    late = lax.all_to_all(late, "seq", 0, 0, tiled=True).reshape(ROWS // 2, HD)
    early = pl.pallas_call(
        attend_early,
        out_shape=pltpu.HBM((SEQ, MID, MOST, HD), BF),
        in_specs=[SMEM] + [VMEM] * (1 + SEQ),
        out_specs=HBM,
        scratch_shapes=[pltpu.VMEM((SEQ, REST, 2 * HD), BF)] + scratch,
        compiler_params=params(16),
        name="attend_early",
        cost_estimate=estimate(4 * MID * BLOCK * 2 * BLOCK * HD, 8),
    )(place, got, *parts)
    early = lax.all_to_all(early, "seq", 0, 0, tiled=True)
    early = early.reshape(ROWS // 2, HD)
    taken = pl.pallas_call(
        take_rows,
        out_shape=shape((TOK, HD), BF),
        in_specs=[SMEM, VMEM, VMEM],
        out_specs=VMEM,
        scratch_shapes=[pltpu.VMEM((ROWS, 1, HD), F32), pltpu.VMEM((TOK, 1, HD), F32)],
        compiler_params=params(10),
        name="take_rows",
        cost_estimate=estimate(0, 8),
    )(index, early, late)
    all_heads = lax.all_to_all(
        taken.reshape(HEADS, HD, HD), ("hx", "hz"), 0, 0, tiled=True
    )
    whole = lambda *dims: pl.BlockSpec(dims, lambda n: (0,) * len(dims))
    w_specs = [
        pl.BlockSpec((depth, COLS), lambda n: (0, n)) for depth in (512, 512, 512, 256, 256)
    ]
    return pl.pallas_call(
        combine,
        grid=(WIDTH // 2 // COLS,),
        out_shape=shape((HD, WIDTH), BF),
        in_specs=[SMEM, whole(HEADS, HD, HD)] + w_specs * 2 + [whole(HD, WIDTH)],
        out_specs=whole(HD, WIDTH),
        scratch_shapes=[pltpu.VMEM((HD, WIDTH), BF)],
        compiler_params=params(16),
        name="combine",
        cost_estimate=estimate(2 * HD * WIDTH * WIDTH, 10),
    )(place, all_heads, *w_near, *w_far, own)


def solution(mesh):
    grid = Mesh(mesh.devices.reshape(SEQ, SIDE, SIDE), ("seq", "hx", "hz"))
    head = ("hx", "hz")
    in_specs = (
        P("seq", head),
        P(None, head),
        P(None, head),
        P(None, head),
        P(head, None),
        P("seq", head),
        P("seq", head),
    )
    out_specs = P(("seq", "hx", "hz"), None)
    return jax.shard_map(sublayer, mesh=grid, in_specs=in_specs, out_specs=out_specs, check_vma=False)
```

```python
import math

import jax
import jax.numpy as jnp
from jax import lax
from jax.experimental import pallas as pl
from jax.experimental.pallas import tpu as pltpu
from jax.sharding import Mesh, PartitionSpec as P


HD = 128
BLOCK = 512
TOK = 2048
HALF = TOK // 2
SEQ = 8
SIDE = 4
HEADS = 16
WIDTH = 2048
BLK = 8
MOST = 64
ROWS = SEQ * BLK * MOST
MID = BLK // 2
TOLD = (BLK - MID + 1 + (BLK - MID) // 2) * MOST
SENT = TOLD + 16
REST = (MID - 1 + 1 + MID // 2) * MOST
LINE = 4
EMPTY = 1 << 20
POS = 1 << 14
OFFSETS = (0, -1, 1, 2)
SCALE = HD ** (-0.5) * math.log2(math.e)
BF = jnp.bfloat16
F32 = jnp.float32


VMEM = pl.BlockSpec(memory_space=pltpu.VMEM)
SMEM = pl.BlockSpec(memory_space=pltpu.SMEM)
HBM = pl.BlockSpec(memory_space=pltpu.HBM)


def params(mib):
    return pltpu.CompilerParams(vmem_limit_bytes=mib * 1024 * 1024)


def ring(by):
    return [(i, (i + by) % SIDE) for i in range(SIDE)]


def shift(piece, axis, by):
    return lax.ppermute(piece, axis, ring(by))


def ring_gather(piece, axis):
    back = shift(piece, axis, 1)
    ahead = shift(piece, axis, -1)
    half = piece.shape[0] // 2
    far_low = shift(back[:half], axis, 1)
    far_high = shift(ahead[half:], axis, -1)
    return back, ahead, far_low, far_high


def gather_near(part, first, second):
    back, ahead, far_low, far_high = ring_gather(part, first)
    low = jnp.concatenate([part, back], 0)
    high = jnp.concatenate([ahead, far_low, far_high], 0)
    back_low = shift(low, second, 1)
    ahead_low = shift(low, second, -1)
    ahead_high = shift(high, second, -1)
    back_high = shift(high, second, 1)
    return low, high, back_low, back_high, ahead_low, ahead_high


def gather_far(near, second):
    return (shift(near[2], second, 1), shift(near[5], second, -1))


def wrap(index, by):
    return lax.rem(index + (by + SIDE), SIDE)


def slice_of(place_ref, swapped, outer, inner):
    x, z = place_ref[0], place_ref[1]
    if swapped:
        return wrap(x, outer) * SIDE + wrap(z, inner)
    return wrap(x, inner) * SIDE + wrap(z, outer)


def piece_list(refs, outers):
    return [
        (refs[2 * n + m // 2], m % 2, outer, inner)
        for n, outer in enumerate(outers)
        for m, inner in enumerate(OFFSETS)
    ]


def fill_weights(place_ref, weights, target, swapped, outers):
    row = 0
    for outer in outers:
        for inner in OFFSETS:
            src = pl.multiple_of(slice_of(place_ref, swapped, outer, inner) * HD, HD)
            for n, w in enumerate(weights):
                target[row : row + HD, n * HD : (n + 1) * HD] = w[pl.ds(src, HD), :]
            row += HD


def pick_own(place_ref, halves, own_ref):
    head = place_ref[0] * SIDE + place_ref[1]
    per = HALF // HD
    for swapped, pieces in halves:
        row = head - per if swapped else head

        @pl.when((head >= per) if swapped else (head < per))
        def _():
            for ref, at, outer, inner in pieces:
                col = pl.multiple_of(slice_of(place_ref, swapped, outer, inner) * HD, HD)
                rows = pl.multiple_of(at * HALF + row * HD, HD)
                own_ref[:, pl.ds(col, HD)] = ref[pl.ds(rows, HD), :]


TILE = 256


def multiply(pieces, base, w, finish):
    def step(i, carry):
        lhs = jnp.concatenate(
            [
                ref[pl.ds(pl.multiple_of(at * HALF + i * TILE, TILE), TILE), :]
                for ref, at, _, _ in pieces
            ],
            1,
        )
        rows = pl.ds(pl.multiple_of(base + i * TILE, TILE), TILE)
        finish(rows, jnp.dot(lhs, w[...], preferred_element_type=F32))
        return carry

    lax.fori_loop(0, HALF // TILE, step, 0)


def project_near(place_ref, wq, wk, wv, *refs):
    acc_ref, own_ref, wa, wb = refs[12:]
    a, b = piece_list(refs[:6], OFFSETS[:3]), piece_list(refs[6:12], OFFSETS[:3])
    fill_weights(place_ref, (wq, wk, wv), wa, False, OFFSETS[:3])
    fill_weights(place_ref, (wq, wk, wv), wb, True, OFFSETS[:3])

    def finish(rows, total):
        acc_ref[rows, :] = total

    multiply(a, 0, wa, finish)
    multiply(b, HALF, wb, finish)
    pick_own(place_ref, ((False, a), (True, b)), own_ref)


def scatter_rows(index_ref, src, pad):
    def step(i, carry):
        for k in range(16):
            t = i * 16 + k
            pad[index_ref[t]] = src[t]
        return carry

    lax.fori_loop(0, TOK // 16, step, 0)


def project_far(place_ref, index_ref, wq, wk, wv, told_ref, acc, own_in, a0, a1, b0, b1, *refs):
    out_ref, rest_refs, own_out = refs[0], refs[1 : 1 + SEQ], refs[1 + SEQ]
    wa, wb, rows, pad, full, rest, own_ref, sems, rest_sems, own_sem = refs[2 + SEQ :]
    a, b = piece_list((a0, a1), OFFSETS[3:]), piece_list((b0, b1), OFFSETS[3:])
    fill_weights(place_ref, (wq, wk, wv), wa, False, OFFSETS[3:])
    fill_weights(place_ref, (wq, wk, wv), wb, True, OFFSETS[3:])

    def finish(at, total):
        total = (acc[at, :] + total).astype(BF).astype(F32)
        twice = pl.multiple_of(at.start * (ROWS // TOK), TILE)
        pad[pl.ds(twice, TILE * ROWS // TOK)] = jnp.zeros((TILE * ROWS // TOK, LINE, HD), F32)
        flat = rows.reshape(TOK * LINE, HD)
        start = pl.multiple_of(at.start * LINE, LINE)
        for k in range(3):
            flat[pl.ds(start + k, TILE, stride=LINE), :] = total[:, k * HD : (k + 1) * HD]
        flat[pl.ds(start + 3, TILE, stride=LINE), :] = told_ref[at, :]

    multiply(a, 0, wa, finish)
    multiply(b, HALF, wb, finish)
    own_ref[...] = own_in[...]
    pick_own(place_ref, ((False, a), (True, b)), own_ref)
    keep = pltpu.make_async_copy(own_ref, own_out, own_sem)
    keep.start()
    scatter_rows(index_ref, rows, pad)
    flat = pad.reshape(ROWS * LINE, HD)

    def line(o, b, *kinds):
        at = (o * BLK + b) * MOST * LINE
        return jnp.concatenate(
            [flat[pl.ds(at + k, MOST, stride=LINE), :] for k in kinds], 1
        ).astype(BF)

    def put(target, o, n, value):
        target[o, n * MOST : (n + 1) * MOST, :] = value

    def queries(o, b):
        return jnp.concatenate([line(o, b, 0), line(o, b + 1, 0)], 1)

    lane = lax.broadcasted_iota(jnp.int32, (MOST, HD), 1)
    slot = lax.broadcasted_iota(jnp.int32, (MOST, HD), 0)

    def told(o, b, shift):
        at = (o * BLK + b) * MOST * LINE + 3
        return jnp.where(lane == slot + shift, flat[pl.ds(at, MOST, stride=LINE), :], 0.0)

    def told_pair(o, b):
        return jnp.sum(told(o, b, 0) + told(o, b + 1, MOST), axis=0, keepdims=True)

    def digits(o):
        halo = told(o, -1, 0) if o else jnp.zeros((MOST, HD), F32)
        halo = jnp.sum(halo, axis=0, keepdims=True)
        values = [
            jnp.concatenate([told_pair(o, 0), told_pair(o, 2)], 1),
            jnp.concatenate([told_pair(o, 4), told_pair(o, 6)], 1),
            jnp.concatenate([halo, jnp.zeros_like(halo)], 1),
        ]
        high = [jnp.floor(v * (1.0 / 65536)) for v in values]
        left = [v - h * 65536.0 for v, h in zip(values, high)]
        middle = [jnp.floor(v * (1.0 / 256)) for v in left]
        low = [v - m * 256.0 for v, m in zip(left, middle)]
        unused = jnp.zeros((SENT - TOLD - 9, 2 * HD), F32)
        return jnp.concatenate(low + middle + high + [unused], 0).astype(BF)

    def send(o):
        return pltpu.make_async_copy(full.at[o], out_ref.at[o], sems.at[o])

    def send_rest(d):
        o = lax.rem(place_ref[3] + d, SEQ)
        return pltpu.make_async_copy(rest.at[o], rest_refs[d], rest_sems.at[d])

    for o in range(SEQ):
        for n in range(MID - 1, BLK):
            put(full, o, n - (MID - 1), line(o, n, 1, 2))
        for n in range(MID, BLK, 2):
            put(full, o, BLK - MID + 1 + (n - MID) // 2, queries(o, n))
        full[o, TOLD:, :] = digits(o)
        send(o).start()
    for o in range(SEQ):
        for n in range(MID - 1):
            put(rest, o, n, line(o, n, 1, 2))
        put(rest, o, MID - 1, line(o, -1, 1, 2) if o else jnp.zeros((MOST, 2 * HD), BF))
        for n in range(0, MID, 2):
            put(rest, o, MID + n // 2, queries(o, n))
    for d in range(SEQ):
        send_rest(d).start()
    for o in range(SEQ):
        send(o).wait()
    for d in range(SEQ):
        send_rest(d).wait()
    keep.wait()


QT = 128


def told_lines(got):
    digits = got[:, TOLD:, :].astype(F32)
    value = digits[:, 0:3] + digits[:, 3:6] * 256.0 + digits[:, 6:9] * 65536.0
    value = jnp.where(value > 0.0, value - 1.0, float(EMPTY))
    lines = []
    for b in range(-1, BLK):
        row, at = (2, 0) if b < 0 else (b // 4, b % 4 * MOST)
        lines.append(
            jnp.concatenate([value[s, row : row + 1, at : at + MOST] for s in range(SEQ)], 1)
        )
    return lines


def attend_blocks(blocks, lines, query_of, pair_of, scores, tops, full, send):
    column = jnp.concatenate(lines[1:], 0).T
    ones = jnp.ones((BLOCK, HD), BF)
    tiles = [(n, i) for n in range(len(blocks)) for i in range(BLOCK // QT)]

    def size(i):
        return QT // MOST * (i + 1), QT * (i + 1)

    def score(t):
        n, i = tiles[t]
        b = blocks[n]
        srcs, wide = size(i)
        base = jnp.floor(jnp.min(lines[b + 1], axis=1, keepdims=True) * (1.0 / POS)) * POS
        earlier = jnp.where(lines[b] >= base, lines[b], float(EMPTY))
        query = query_of(b, srcs)[i * QT :, :]
        mine = column[i * QT : (i + 1) * QT, b : b + 1]
        top = None
        for k, (which, line) in enumerate(((b - 1, earlier), (b, lines[b + 1]))):
            part = lax.dot_general(
                query,
                pair_of(which, srcs)[:, :HD],
                (((1,), (1,)), ((), ())),
                preferred_element_type=F32,
            )
            part = jnp.where(line[:, :wide] <= mine, part, F32(-1e30))
            scores[t % 2][:, k * wide : (k + 1) * wide] = part
            part = jnp.max(part, axis=1, keepdims=True)
            top = part if top is None else jnp.maximum(top, part)
        tops[t % 2][...] = jnp.broadcast_to(top, (QT, HD))

    def finish(t):
        n, i = tiles[t]
        b = blocks[n]
        srcs, wide = size(i)
        mixed = None
        for k, which in enumerate((b - 1, b)):
            top = jnp.concatenate([tops[t % 2][...]] * (wide // HD), 1)
            part = scores[t % 2][:, k * wide : (k + 1) * wide]
            expon = jnp.exp2((part - top) * F32(SCALE)).astype(BF)
            values = jnp.concatenate([pair_of(which, srcs)[:, HD:], ones[:wide]], 1)
            prod = jnp.dot(expon, values, preferred_element_type=F32)
            mixed = prod if mixed is None else mixed + prod
        done = (mixed[:, :HD] / mixed[:, HD:]).astype(BF)
        full[QT // MOST * i : srcs, n] = done.reshape(QT // MOST, MOST, HD)
        if i == BLOCK // QT - 1:
            send(n).start()

    score(0)
    for t in range(len(tiles)):
        if t + 1 < len(tiles):
            score(t + 1)
        finish(t)
    for n in range(len(blocks)):
        send(n).wait()


def rows_of(ref, n, srcs):
    return ref[:srcs, n * MOST : (n + 1) * MOST, :].reshape(srcs * MOST, 2 * HD)


def attend_late(got, out_ref, s0, s1, t0, t1, full, sems):
    def query_of(b, srcs):
        half = b % 2 * HD
        return rows_of(got, BLK - MID + 1 + (b - MID) // 2, srcs)[:, half : half + HD]

    def pair_of(b, srcs):
        return rows_of(got, b - (MID - 1), srcs)

    def send(n):
        return pltpu.make_async_copy(full.at[:, n], out_ref.at[:, n], sems.at[n])

    attend_blocks(
        range(MID, BLK), told_lines(got), query_of, pair_of, (s0, s1), (t0, t1), full, send
    )


def attend_early(place_ref, got, *refs):
    parts, out_ref = refs[:SEQ], refs[SEQ]
    rest, s0, s1, t0, t1, full, sems = refs[SEQ + 1 :]
    for d in range(SEQ):
        rest[lax.rem(place_ref[3] + (SEQ - d), SEQ)] = parts[d][...]

    def query_of(b, srcs):
        half = b % 2 * HD
        return rows_of(rest, MID + b // 2, srcs)[:, half : half + HD]

    def pair_of(b, srcs):
        if b == MID - 1:
            return rows_of(got, 0, srcs)
        return rows_of(rest, MID - 1 if b < 0 else b, srcs)

    def send(n):
        return pltpu.make_async_copy(full.at[:, n], out_ref.at[:, n], sems.at[n])

    attend_blocks(range(MID), told_lines(got), query_of, pair_of, (s0, s1), (t0, t1), full, send)


def take_rows(index_ref, early_ref, late_ref, out_ref, wide, taken):
    flat = wide.reshape(ROWS, HD)
    per = MID * MOST
    for o in range(SEQ):
        for n, ref in enumerate((early_ref, late_ref)):
            at = (2 * o + n) * per
            flat[at : at + per, :] = ref[o * per : (o + 1) * per, :].astype(F32)

    def step(i, carry):
        for k in range(16):
            t = i * 16 + k
            taken[t] = wide[index_ref[t]]
        return carry

    lax.fori_loop(0, TOK // 16, step, 0)
    out_ref[...] = taken.reshape(TOK, HD)[...].astype(BF)


COLS = 256


def combine(place_ref, rows_ref, *refs):
    near, far = refs[: 2 * SIDE], refs[2 * SIDE : 4 * SIDE]
    own_ref, out_ref, lhs = refs[4 * SIDE :]
    n = pl.program_id(0)

    @pl.when(n == 0)
    def _():
        for k, outer in enumerate(OFFSETS):
            for m, inner in enumerate(OFFSETS):
                h = slice_of(place_ref, False, outer, inner)
                col = (k * SIDE + m) * HD
                lhs[:, col : col + HD] = rows_ref[h]

    core = place_ref[2]
    for group, which in ((near, core), (far, 1 - core)):
        total, row = None, 0
        for w in group:
            depth = w.shape[0]
            prod = jnp.dot(lhs[:, row : row + depth], w[...], preferred_element_type=F32)
            total = prod if total is None else total + prod
            row += depth
        col = pl.ds(pl.multiple_of(which * (WIDTH // 2) + n * COLS, COLS), COLS)
        out_ref[:, col] = (total + own_ref[:, col].astype(F32)).astype(BF)


def estimate(flops, mib):
    return pl.CostEstimate(flops=flops, bytes_accessed=mib << 20, transcendentals=0)


def shape(dims, kind):
    return jax.ShapeDtypeStruct(dims, kind)


def sublayer(tokens, w_query, w_key, w_value, w_out, cluster_id, slot_index):
    x, z, seq = lax.axis_index("hx"), lax.axis_index("hz"), lax.axis_index("seq")
    core = lax.rem(seq, 2)
    place = jnp.stack([x, z, core, seq]).astype(jnp.int32)

    slots = slot_index.reshape(TOK)
    index = (slots // BLOCK) * MOST + slots % MOST
    value = cluster_id * POS + 1 + seq * TOK + lax.broadcasted_iota(jnp.int32, (TOK, 1), 0)
    told = jnp.broadcast_to(value.astype(F32), (TOK, HD))

    near_a = gather_near(tokens[:HALF], "hx", "hz")
    near_b = gather_near(tokens[HALF:], "hz", "hx")
    w_half = lax.dynamic_slice_in_dim(w_out, core * (WIDTH // 2), WIDTH // 2, 1)
    w_row = (w_half,) + tuple(shift(w_half, "hx", -by) for by in OFFSETS[1:])

    weights = (w_query, w_key, w_value)
    acc, own = pl.pallas_call(
        project_near,
        out_shape=(shape((TOK, 3 * HD), F32), shape((HD, WIDTH), BF)),
        in_specs=[SMEM] + [VMEM] * 15,
        out_specs=(VMEM, VMEM),
        scratch_shapes=[pltpu.VMEM((12 * HD, 3 * HD), BF)] * 2,
        compiler_params=params(20),
        name="project_near",
        cost_estimate=estimate(2 * TOK * 12 * HD * 3 * HD, 10),
    )(place, *weights, *near_a, *near_b)
    far_a = gather_far(near_a, "hz")
    far_b = gather_far(near_b, "hx")
    sent, *rest, own = pl.pallas_call(
        project_far,
        out_shape=(
            pltpu.HBM((SEQ, SENT, 2 * HD), BF),
            *[pltpu.HBM((REST, 2 * HD), BF)] * SEQ,
            pltpu.HBM((HD, WIDTH), BF),
        ),
        in_specs=[SMEM, SMEM] + [VMEM] * 10,
        out_specs=(HBM,) * (2 + SEQ),
        scratch_shapes=[pltpu.VMEM((4 * HD, 3 * HD), BF)] * 2
        + [
            pltpu.VMEM((TOK, LINE, HD), F32),
            pltpu.VMEM((ROWS, LINE, HD), F32),
            pltpu.VMEM((SEQ, SENT, 2 * HD), BF),
            pltpu.VMEM((SEQ, REST, 2 * HD), BF),
            pltpu.VMEM((HD, WIDTH), BF),
            pltpu.SemaphoreType.DMA((SEQ,)),
            pltpu.SemaphoreType.DMA((SEQ,)),
            pltpu.SemaphoreType.DMA,
        ],
        compiler_params=params(28),
        name="project_far",
        cost_estimate=estimate(2 * TOK * 4 * HD * 3 * HD, 24),
    )(place, index, *weights, told, acc, own, *far_a, *far_b)
    got = lax.all_to_all(sent, "seq", 0, 0, tiled=True)
    parts = [rest[0]]
    for d in range(1, SEQ):
        parts.append(lax.ppermute(rest[d], "seq", [(i, (i + d) % SEQ) for i in range(SEQ)]))

    w_row, _ = lax.optimization_barrier((w_row, own))
    w_low, w_high = jnp.concatenate(w_row[:2], 0), jnp.concatenate(w_row[2:], 0)
    low_back = shift(w_low, "hz", 1)
    high_ahead = shift(w_high, "hz", -1)
    low_ahead = shift(w_low, "hz", -1)
    high_back = shift(w_high, "hz", 1)
    far_low = shift(low_back, "hz", 1)
    far_high = shift(high_ahead, "hz", -1)
    w_near = (w_low, w_high, low_back, high_back, low_ahead, high_ahead, far_low, far_high)
    w_far = []
    for w in w_near:
        w_far.append(lax.ppermute(w, "seq", [(i, i ^ 1) for i in range(SEQ)]))

    scratch = [
        *[pltpu.VMEM((QT, 2 * BLOCK), F32)] * 2,
        *[pltpu.VMEM((QT, HD), F32)] * 2,
        pltpu.VMEM((SEQ, MID, MOST, HD), BF),
        pltpu.SemaphoreType.DMA((MID,)),
    ]
    late = pl.pallas_call(
        attend_late,
        out_shape=pltpu.HBM((SEQ, MID, MOST, HD), BF),
        in_specs=[VMEM],
        out_specs=HBM,
        scratch_shapes=scratch,
        compiler_params=params(12),
        name="attend_late",
        cost_estimate=estimate(4 * MID * BLOCK * 2 * BLOCK * HD, 6),
    )(got)
    late = lax.all_to_all(late, "seq", 0, 0, tiled=True)
    late = late.reshape(ROWS // 2, HD)
    early = pl.pallas_call(
        attend_early,
        out_shape=pltpu.HBM((SEQ, MID, MOST, HD), BF),
        in_specs=[SMEM] + [VMEM] * (1 + SEQ),
        out_specs=HBM,
        scratch_shapes=[pltpu.VMEM((SEQ, REST, 2 * HD), BF)] + scratch,
        compiler_params=params(16),
        name="attend_early",
        cost_estimate=estimate(4 * MID * BLOCK * 2 * BLOCK * HD, 8),
    )(place, got, *parts)
    early = lax.all_to_all(early, "seq", 0, 0, tiled=True)
    early = early.reshape(ROWS // 2, HD)
    taken = pl.pallas_call(
        take_rows,
        out_shape=shape((TOK, HD), BF),
        in_specs=[SMEM, VMEM, VMEM],
        out_specs=VMEM,
        scratch_shapes=[pltpu.VMEM((ROWS, 1, HD), F32), pltpu.VMEM((TOK, 1, HD), F32)],
        compiler_params=params(10),
        name="take_rows",
        cost_estimate=estimate(0, 8),
    )(index, early, late)
    all_heads = lax.all_to_all(
        taken.reshape(HEADS, HD, HD), ("hx", "hz"), 0, 0, tiled=True
    )
    whole = lambda *dims: pl.BlockSpec(dims, lambda n: (0,) * len(dims))
    w_specs = [pl.BlockSpec((SIDE // 2 * HD, COLS), lambda n: (0, n))] * (2 * SIDE)
    return pl.pallas_call(
        combine,
        grid=(WIDTH // 2 // COLS,),
        out_shape=shape((HD, WIDTH), BF),
        in_specs=[SMEM, whole(HEADS, HD, HD)] + w_specs * 2 + [whole(HD, WIDTH)],
        out_specs=whole(HD, WIDTH),
        scratch_shapes=[pltpu.VMEM((HD, WIDTH), BF)],
        compiler_params=params(16),
        name="combine",
        cost_estimate=estimate(2 * HD * WIDTH * WIDTH, 10),
    )(place, all_heads, *w_near, *w_far, own)


def solution(mesh):
    grid = Mesh(mesh.devices.reshape(SEQ, SIDE, SIDE), ("seq", "hx", "hz"))
    head = ("hx", "hz")
    in_specs = (
        P("seq", head),
        P(None, head),
        P(None, head),
        P(None, head),
        P(head, None),
        P("seq", head),
        P("seq", head),
    )
    out_specs = P(("seq", "hx", "hz"), None)
    return jax.shard_map(sublayer, mesh=grid, in_specs=in_specs, out_specs=out_specs, check_vma=False)
```
